32 devices in a mesh: row: 8 (over z, x), col: 4 (over y, core).
Axes of the slice: x: 2, y: 2, z: 4, core: 2. Of those that a mesh axis runs over, the one named last changes fastest.
Arguments:
- density: float32 [3, 524288], P(None, ('row', 'col')), may hold values from -6 to 6
- interp_weight: float32 [27, 524288], P(None, ('row', 'col')), may hold values from -1.2 to 1.2
- proj_weight: float32 [27, 524288], P(None, ('row', 'col')), may hold values from -1.2 to 1.2
- stencil_corner: int32 [3, 4096], P(None, ('row', 'col')), may hold values from 0 to 253, as said below
- near_tiles: bfloat16 [384, 3, 3, 128, 128], P(('row', 'col')), may hold values from -0.1875 to 0.1875
- pair_target: int32 [384], P(('row', 'col')), may hold values from 0 to 127
- pair_landing: int32 [384], P(('row', 'col')), may hold values from 0 to 127
- pair_count: int32 [32], P(('row', 'col')), may hold values from 4 to 12, as said below
Outputs:
- traction_adjoint: float32 [3, 524288], P(None, ('row', 'col'))
The draws below stay inside these ranges and needn't reach their ends.
Inputs may be any that keep to these rules, and one draw needn't show every extreme that they name: `stencil_corner`: the stencil of a cluster held by the device with row index r and col index c lies in cells r * 32 to r * 32 + 31 of the first dimension and c * 64 to c * 64 + 63 of the second; every stencil lies inside the grid. `pair_count`: slots at or beyond a device's count are padding; the most is reached on some device in every draw.
All inputs are finite; a program needn't handle non-finite values.
Results may differ from the reference program's by a relative error of at most 0.0003.
Values sent between devices are 32-bit elements; how exact they have to be, the bound alone decides.
No kernel may reach another device: no remote copies, remote signals or barrier semaphores. Data moves between devices by JAX's collectives and lax.ppermute only.
A program may use at most 128 MiB of HBM per device.

```python
import math
import jax
import jax.numpy as jnp
from jax import lax

G = 256
PC = 128
STENCIL = 27
CL_DEV = 128
PAIR_GROUP = 4
CLUSTERS = 4096
PANELS = 524288
PAIRS = 384
N_ROW = 8
N_COL = 4
DEVICES = 32


def pair_tables(key):
    base_key = jax.random.fold_in(key, 11)
    subkeys = jax.random.split(base_key, 4)
    slot_count = 3 * PAIR_GROUP
    target = jax.random.randint(subkeys[0], (DEVICES, slot_count), 0, CL_DEV)
    landing = jax.random.randint(subkeys[1], (DEVICES, slot_count), 0, CL_DEV)
    count_draws = jax.random.randint(subkeys[2], (2, DEVICES), 0, 2 * PAIR_GROUP + 1)
    counts = PAIR_GROUP + jnp.min(count_draws, axis=0)
    chosen = jax.random.randint(subkeys[3], (), 0, DEVICES)
    counts = counts.at[chosen].set(3 * PAIR_GROUP).astype(jnp.int32)
    return (target.reshape(-1).astype(jnp.int32), landing.reshape(-1).astype(jnp.int32), counts)


def draw_pair_target(key, part):
    return pair_tables(key)[0]


def draw_pair_landing(key, part):
    return pair_tables(key)[1]


def draw_pair_count(key, part):
    return pair_tables(key)[2]


def draw_stencil_corner(key, part):
    base_key = jax.random.fold_in(key, 5)
    key_first, key_second, key_third = jax.random.split(base_key, 3)
    holder = jnp.arange(CLUSTERS, dtype=jnp.int32) // CL_DEV
    row_of = holder // N_COL
    col_of = holder % N_COL
    slab_first = G // N_ROW
    slab_second = G // N_COL
    first_corner = row_of * slab_first + jax.random.randint(key_first, (CLUSTERS,), 0, slab_first - 2)
    second_corner = col_of * slab_second + jax.random.randint(key_second, (CLUSTERS,), 0, slab_second - 2)
    third_corner = jax.random.randint(key_third, (CLUSTERS,), 0, G - 2)
    return jnp.stack([first_corner, second_corner, third_corner]).astype(jnp.int32)


def levels(key, shape, cuts, smallest, high):
    def one(axis_at, blocks):
        steps = jax.random.uniform(jax.random.fold_in(jax.random.fold_in(key, 6), axis_at), (blocks,), jnp.float32, smallest / len(cuts), high / len(cuts))
        return jnp.repeat(jnp.exp(steps), shape[axis_at] // blocks).reshape((-1,) + (1,) * (len(shape) - axis_at - 1))

    gain = one(*cuts[0])
    for cut in cuts[1:]:
        gain = gain * one(*cut)
    return gain


def centred(stream_key, dims, scale, reach, cuts=(), held_as=jnp.bfloat16):
    values = scale * jax.random.normal(stream_key, dims, jnp.float32)
    if cuts:
        values = values * levels(stream_key, dims, cuts, -0.22, 0.18)
    return jnp.clip(values, -reach, reach).astype(held_as)


def setup_inputs(seed: int = 0) -> dict:
    seeds = jax.random.split(jax.random.key(seed), 9)
    return {
        "density": centred(seeds[0], (3, PANELS), 1.0, 6.0, ((1, 32),), jnp.float32),
        "interp_weight": centred(seeds[1], (STENCIL, PANELS), 0.19245, 1.2, ((1, 32),), jnp.float32),
        "proj_weight": centred(seeds[2], (STENCIL, PANELS), 0.19245, 1.2, ((1, 32),), jnp.float32),
        "stencil_corner": draw_stencil_corner(jax.random.fold_in(seeds[8], 71), 0),
        "near_tiles": centred(seeds[4], (PAIRS, 3, 3, PC, PC), (9 * PC) ** -0.5, 0.1875, ((0, 32),)),
        "pair_target": draw_pair_target(jax.random.fold_in(seeds[8], 71), 0),
        "pair_landing": draw_pair_landing(jax.random.fold_in(seeds[8], 71), 0),
        "pair_count": draw_pair_count(jax.random.fold_in(seeds[8], 71), 0),
    }


precise = lax.Precision.HIGHEST
screen_shift = 0.5

def wavenumbers(count, offset, length):
    indices = offset + jnp.arange(count, dtype=jnp.int32)
    wave_values = jnp.where(indices < length // 2, indices, indices - length).astype(jnp.float32)
    keep_mask = (indices != length // 2).astype(jnp.float32)
    return (wave_values, keep_mask)

def screen_project(spectra, first_pair, second_pair, third_pair, factor):
    kfirst, keep_first = first_pair
    ksecond, keep_second = second_pair
    kthird, keep_third = third_pair
    squared = kfirst * kfirst + ksecond * ksecond + kthird * kthird
    weighting = factor * keep_first * keep_second * keep_third / (squared + screen_shift)
    floor_sq = jnp.maximum(squared, 1.0)
    result = []
    for spectral in spectra:
        inner_sum = (kfirst * spectral[0] + ksecond * spectral[1] + kthird * spectral[2]) / floor_sq
        stacked = jnp.stack([spectral[0] - kfirst * inner_sum, spectral[1] - ksecond * inner_sum, spectral[2] - kthird * inner_sum])
        result.append(stacked * weighting)
    return result

def reference(density, interp_weight, proj_weight, stencil_corner, near_tiles, pair_target, pair_landing, pair_count):
    charges = density.reshape(3, CLUSTERS, PC)
    weights_in = interp_weight.reshape(STENCIL, CLUSTERS, PC)
    weights_out = proj_weight.reshape(STENCIL, CLUSTERS, PC)
    offsets = jnp.arange(STENCIL, dtype=jnp.int32)
    cell_index = ((stencil_corner[0][:, None] + offsets // 9) * G + stencil_corner[1][:, None] + offsets // 3 % 3) * G + stencil_corner[2][:, None] + offsets % 3
    cell_index = cell_index.astype(jnp.int32)
    spread = jnp.einsum('ckp,skp->cks', charges, weights_in, precision=precise)
    charge_grid = jnp.zeros((3, G * G * G), jnp.float32).at[:, cell_index.reshape(-1)].add(spread.reshape(3, -1)).reshape(3, G, G, G)
    spectrum = jnp.fft.fftn(charge_grid, axes=(1, 2, 3))
    wave_pair = wavenumbers(G, 0, G)
    first_pair = tuple((member[:, None, None] for member in wave_pair))
    second_pair = tuple((member[None, :, None] for member in wave_pair))
    third_pair = tuple((member[None, None, :] for member in wave_pair))
    factor = 1.0 / math.sqrt(PANELS)
    real_part, imag_part = screen_project((jnp.real(spectrum), jnp.imag(spectrum)), first_pair, second_pair, third_pair, factor)
    potential = jnp.real(jnp.fft.ifftn(lax.complex(real_part, imag_part), axes=(1, 2, 3))) * float(G ** 3)
    sampled = potential.reshape(3, -1)[:, cell_index]
    far_term = jnp.einsum('cks,skp->ckp', sampled, weights_out, precision=precise)
    rounded = charges.astype(jnp.bfloat16).astype(jnp.float32)
    per_device = 3 * PAIR_GROUP
    tiles_by_dev = near_tiles.reshape(DEVICES, per_device, 3, 3, PC, PC)
    target_by_dev = pair_target.reshape(DEVICES, per_device)
    landing_by_dev = pair_landing.reshape(DEVICES, per_device)
    position = jnp.arange(per_device, dtype=jnp.int32)
    shift_code = jnp.where(position < PAIR_GROUP, 0, jnp.where((position - PAIR_GROUP) % 2 == 0, -1, 1)).astype(jnp.int32)

    def visit_device(near_total, device):
        block_tiles = lax.dynamic_index_in_dim(tiles_by_dev, device, keepdims=False).astype(jnp.float32)
        targets = (device * CL_DEV + lax.dynamic_index_in_dim(target_by_dev, device, keepdims=False)).astype(jnp.int32)
        picked = rounded[:, targets, :]
        partial_value = jnp.einsum('qabij,aqi->qbj', block_tiles, picked, precision=precise)
        live_mask = position < pair_count[device]
        row_of = device // N_COL
        col_of = device % N_COL
        holder = ((row_of + shift_code) % N_ROW * N_COL + col_of).astype(jnp.int32)
        sources = (holder * CL_DEV + landing_by_dev[holder, position]).astype(jnp.int32)
        masked = jnp.where(live_mask[:, None, None], partial_value, jnp.zeros_like(partial_value))
        near_total = near_total.at[:, sources, :].add(jnp.transpose(masked, (1, 0, 2)))
        return (near_total, None)
    near_term, unused = lax.scan(visit_device, jnp.zeros((3, CLUSTERS, PC), jnp.float32), jnp.arange(DEVICES, dtype=jnp.int32))
    return (far_term + near_term).reshape(3, PANELS)
```

```python
import math

import jax
import jax.numpy as jnp
import numpy as np
from jax import lax
from jax.experimental import pallas as pl
from jax.experimental.pallas import tpu as pltpu
from jax.sharding import PartitionSpec as P

G = 256
HALF = G // 2
STENCIL = 27
SIDE = 3
AXES = ("row", "col")

precise = lax.Precision.HIGHEST
screen_shift = 0.5


def padded(cells, sides, width):
    for axis, dim in sides:
        count = lax.axis_size(axis)
        head = lax.slice_in_dim(cells, 0, width, axis=dim)
        tail = lax.slice_in_dim(cells, cells.shape[dim] - width, cells.shape[dim], axis=dim)
        cells = jnp.concatenate(
            [
                lax.ppermute(tail, axis, [(i, (i + 1) % count) for i in range(count)]),
                cells,
                lax.ppermute(head, axis, [((i + 1) % count, i) for i in range(count)]),
            ],
            axis=dim,
        )
    return cells


def near_field(charges, near_tiles, pair_target, pair_landing, pair_count):
    clusters, panels = charges.shape[1:]
    rounded = charges.astype(jnp.bfloat16)
    slot_total = pair_target.shape[0]
    slot_group = slot_total // 3
    picked = rounded[:, pair_target, :]
    partial_value = jnp.einsum(
        "qabij,aqi->qbj", near_tiles, picked, preferred_element_type=jnp.float32
    )
    live_mask = jnp.arange(slot_total, dtype=jnp.int32) < pair_count[0]
    partial_value = jnp.where(
        live_mask[:, None, None], partial_value, jnp.zeros_like(partial_value)
    )
    leaving = partial_value[slot_group:].reshape(slot_group, 2, 3, panels)
    arrived = padded(leaving, (("row", 1),), 1)
    crossing = jnp.stack([arrived[:, 3], arrived[:, 0]], axis=1).reshape(2 * slot_group, 3, panels)
    incoming = jnp.concatenate([partial_value[:slot_group], crossing], axis=0)
    landing_hot = (pair_landing[:, None] == jnp.arange(clusters, dtype=jnp.int32)[None, :]).astype(
        jnp.float32
    )
    return jnp.einsum("qk,qbj->bkj", landing_hot, incoming, precision=precise)


def half_tables():
    cells = np.arange(HALF)
    parts = []
    for parity in range(2):
        product = cells[:, None] * (2 * cells[None, :] + parity) % G
        angles = product * (2.0 * np.pi / G)
        cosines, sines = np.cos(angles), np.sin(angles)
        table = np.block([[cosines, -sines], [sines, cosines]]).astype(np.float32)
        high = table.astype(jnp.bfloat16)
        low = (table - high.astype(np.float32)).astype(jnp.bfloat16)
        parts.append(np.stack([high, low]))
    return np.stack(parts)


def split(values):
    high = values.astype(jnp.bfloat16)
    low = (values - high.astype(jnp.float32)).astype(jnp.bfloat16)
    return high, low


def dot(left, right):
    return jnp.dot(left, right, preferred_element_type=jnp.float32)


def three_pass(left_high, left_low, right_high, right_low):
    return (
        dot(left_high, right_low) + dot(left_low, right_high) + dot(left_high, right_high)
    )


def scatter_kernel(cols, stencils, phases, out, spread, hot, total):
    parts, slab, _ = out.shape
    clusters = stencils.shape[2]
    corner = pl.program_id(0) * slab

    def block(c, carry):
        first = stencils[c, 3 * STENCIL : 3 * STENCIL + 1, :] - corner.astype(jnp.float32)
        second = stencils[c, 3 * STENCIL + 1 : 3 * STENCIL + 2, :]
        rows = lax.broadcasted_iota(jnp.int32, (G, clusters), 0).astype(jnp.float32)
        first_wide = jnp.broadcast_to(first, (2 * parts, clusters)).astype(jnp.bfloat16)
        for y in range(SIDE):
            lanes = pl.ds(pl.multiple_of((c * SIDE + y) * clusters, clusters), clusters)
            hot[:, lanes] = jnp.where(rows == second + y, 1.0, 0.0).astype(jnp.bfloat16)
            tiles = []
            for x in range(SIDE):
                modes = []
                for a in range(3):
                    at = a * STENCIL + x * 9 + y * 3
                    modes.append(
                        sum(stencils[c, at + z : at + z + 1, :] * phases[c, z] for z in range(SIDE))
                    )
                modes = jnp.concatenate(modes, axis=0)
                low = modes - modes.astype(jnp.bfloat16).astype(jnp.float32)
                tiles.append(jnp.concatenate([modes, low], axis=0).astype(jnp.bfloat16))
            blank = jnp.zeros_like(tiles[0])
            for cell in range(slab):
                value = blank
                for x in range(SIDE):
                    value = jnp.where(
                        first_wide == jnp.asarray(cell - x, jnp.bfloat16), tiles[x], value
                    )
                spread[cell, :, lanes] = value
        return carry

    lax.fori_loop(0, cols, block, 0)
    result = lax.dot_general(
        spread[...].reshape(slab * 2 * parts, hot.shape[1]),
        hot[...],
        (((1,), (1,)), ((), ())),
        preferred_element_type=jnp.float32,
    )
    for side in range(2):
        total[side] = result[:, side * HALF : (side + 1) * HALF]
    for side in range(2):
        for v in range(parts):
            out[v, :, side * HALF : (side + 1) * HALF] = (
                total[side, pl.ds(v, slab, stride=2 * parts), :]
                + total[side, pl.ds(parts + v, slab, stride=2 * parts), :]
            )


def dft_kernel(signs, thirds, field, tx, txt, ty, tyt, out, lines, modes, high, low):
    pars = ty.shape[0]
    width = pars * HALF

    def stage(values, at):
        high[at], low[at] = split(values)

    for p in range(pars):
        for a in range(3):
            for part in range(2):
                stage(
                    field[a, 0, part, :, :HALF] + signs[p] * field[a, 0, part, :, HALF:],
                    (slice(a * G, (a + 1) * G), slice(part * HALF, (part + 1) * HALF)),
                )
        for a in range(3):
            rows = slice(a * G, (a + 1) * G)
            result = three_pass(high[rows], low[rows], ty[p, 0], ty[p, 1])
            for part in range(2):
                lines[a, part, :, p * HALF : (p + 1) * HALF] = result[
                    :, part * HALF : (part + 1) * HALF
                ]
    for a in range(3):
        for q in range(2):
            rows = slice((2 * a + q) % 3 * G, ((2 * a + q) % 3 + 1) * G)
            for part in range(2):
                top, bottom = lines[a, part, :HALF], lines[a, part, HALF:]
                at = rows.start + part * HALF
                stage(top - bottom if q else top + bottom, (slice(at, at + HALF), slice(0, width)))
            result = three_pass(txt[q, 0], txt[q, 1], high[rows, :width], low[rows, :width])
            for part in range(2):
                modes[a, part, q * HALF : (q + 1) * HALF] = result[
                    part * HALF : (part + 1) * HALF
                ]

    m = pl.program_id(0)
    kthird = thirds[0, m]
    scale = thirds[1, m]
    chunk = 16

    def project(i, carry):
        rows = pl.ds(pl.multiple_of(i * chunk, chunk), chunk)
        at = lax.broadcasted_iota(jnp.int32, (chunk, width), 0) + i * chunk
        bin_first = jnp.where(at < HALF, 2 * at, 2 * at - (G - 1))
        lane = lax.broadcasted_iota(jnp.int32, (chunk, width), 1)
        second = []
        for p in range(pars):
            odd = jnp.where(signs[p] < 0.0, 1, 0)
            second.append(2 * (lane[:, p * HALF : (p + 1) * HALF] - p * HALF) + odd)
        bin_second = jnp.concatenate(second, axis=1) if pars > 1 else second[0]
        kept = (bin_first != HALF) & (bin_second != HALF)
        kfirst = jnp.where(bin_first < HALF, bin_first, bin_first - G).astype(jnp.float32)
        ksecond = jnp.where(bin_second < HALF, bin_second, bin_second - G).astype(jnp.float32)
        squared = kfirst * kfirst + ksecond * ksecond + kthird * kthird
        weighting = jnp.where(kept, scale / (squared + screen_shift), 0.0)
        inverse = 1.0 / jnp.maximum(squared, 1.0)
        for part in range(2):
            u, v, w = (modes[a, part, rows, :] for a in range(3))
            inner = (kfirst * u + ksecond * v + kthird * w) * inverse
            lines[0, part, rows, :] = (u - kfirst * inner) * weighting
            lines[1, part, rows, :] = (v - ksecond * inner) * weighting
            lines[2, part, rows, :] = (w - kthird * inner) * weighting
        return carry

    lax.fori_loop(0, G // chunk, project, 0)

    for a in range(3):
        results = []
        for q in range(2):
            rows = slice((2 * a + q) % 3 * G, ((2 * a + q) % 3 + 1) * G)
            for part in range(2):
                at = rows.start + part * HALF
                stage(
                    lines[a, part, q * HALF : (q + 1) * HALF],
                    (slice(at, at + HALF), slice(0, width)),
                )
            results.append(
                three_pass(tx[q, 0], tx[q, 1], high[rows, :width], low[rows, :width])
            )
        for part in range(2):
            even, odd = (r[part * HALF : (part + 1) * HALF] for r in results)
            modes[a, part, :HALF] = even + odd
            modes[a, part, HALF:] = even - odd
    for a in range(3):
        near = far = None
        for p in range(pars):
            rows = slice((2 * a + p) % 3 * G, ((2 * a + p) % 3 + 1) * G)
            for part in range(2):
                stage(
                    modes[a, part, :, p * HALF : (p + 1) * HALF],
                    (rows, slice(part * HALF, (part + 1) * HALF)),
                )
            result = three_pass(high[rows], low[rows], tyt[p, 0], tyt[p, 1])
            near = result if near is None else near + result
            far = signs[p] * result if far is None else far + signs[p] * result
        for part in range(2):
            out[a, 0, part, :, :HALF] = near[:, part * HALF : (part + 1) * HALF]
            out[a, 0, part, :, HALF:] = far[:, part * HALF : (part + 1) * HALF]


def gather_kernel(cols, stencils, phases, field, out, lines, found):
    parts, slab, _ = field.shape
    clusters = stencils.shape[2]
    bins = parts // 3
    span = G // cols
    corner = (pl.program_id(0) * slab).astype(jnp.float32)
    for v in range(parts):
        for side in range(2):
            lines[side, pl.ds(v, slab, stride=parts), :] = field[
                v, :, side * HALF : (side + 1) * HALF
            ]
    for c in range(cols):
        first = stencils[c, 3 * STENCIL : 3 * STENCIL + 1, :] - corner
        second = stencils[c, 3 * STENCIL + 1 : 3 * STENCIL + 2, :]
        rows = lax.broadcasted_iota(jnp.int32, (2 * span, clusters), 0)
        rows = (jnp.where(rows < span, rows, rows - span) + c * span).astype(jnp.float32)
        hot = jnp.concatenate(
            [jnp.where(rows == second + y, 1.0, 0.0) for y in range(SIDE)], axis=1
        ).astype(jnp.bfloat16)
        side, start = divmod(c * span, HALF)
        values = lines[side, :, start : start + span]
        high, low = split(values)
        found[...] = dot(jnp.concatenate([high, low], axis=1), hot)
        wide = jnp.broadcast_to(first, (parts, clusters))
        for y in range(SIDE):
            lanes = slice(y * clusters, (y + 1) * clusters)
            sums = [jnp.zeros((parts, clusters), jnp.float32) for _ in range(SIDE)]
            for cell in range(slab):
                value = found[cell * parts : (cell + 1) * parts, lanes]
                for x in range(SIDE):
                    if 0 <= cell - x <= slab - SIDE:
                        sums[x] = jnp.where(wide == (cell - x), value, sums[x])
            for x in range(SIDE):
                for a in range(3):
                    mode = sums[x][a * bins : (a + 1) * bins]
                    for z in range(SIDE):
                        at = a * STENCIL + x * 9 + y * 3 + z
                        out[c, at : at + 1, :] = jnp.sum(
                            mode * phases[c, z], axis=0, keepdims=True
                        )


def per_device(
    density,
    interp_weight,
    proj_weight,
    stencil_corner,
    near_tiles,
    pair_target,
    pair_landing,
    pair_count,
):
    clusters = stencil_corner.shape[1]
    panels = density.shape[1] // clusters
    rows_total = lax.axis_size("row")
    cols_total = lax.axis_size("col")
    devices = rows_total * cols_total
    device = lax.axis_index("row") * cols_total + lax.axis_index("col")
    slab = G // rows_total
    kept_bins = G // 2
    third_parts = min(devices, kept_bins)
    second_parts = devices // third_parts
    pars = 2 // second_parts
    third_live = kept_bins // third_parts
    bins = max(4, third_live)
    parts = 3 * 2 * bins
    width = pars * HALF
    f32, bf16 = jnp.float32, jnp.bfloat16

    charges = density.reshape(3, clusters, panels)
    weights_in = interp_weight.reshape(STENCIL, clusters, panels)
    weights_out = proj_weight.reshape(STENCIL, clusters, panels)
    spread = jnp.einsum("ckp,skp->csk", charges, weights_in, precision=precise)
    packed = jnp.concatenate(
        [spread.reshape(3 * STENCIL, clusters), stencil_corner.astype(f32)], axis=0
    )
    height = 3 * STENCIL + 3
    everyone = lax.all_to_all(
        jnp.broadcast_to(packed[None], (devices, height, clusters)), AXES, 0, 0, tiled=True
    )

    step = jnp.arange(bins, dtype=jnp.int32)
    third_bins = (device // second_parts) * third_live + step
    live = (step < third_live).astype(f32)
    factor = 1.0 / math.sqrt(density.shape[1] * devices)
    fold = jnp.where(third_bins == 0, 1.0, 2.0).astype(f32)
    thirds = jnp.stack([third_bins.astype(f32), live * fold * factor])
    first_parity = device % second_parts
    signs = 1.0 - 2.0 * (first_parity + jnp.arange(pars, dtype=jnp.int32)).astype(f32)

    shape = (devices, SIDE, bins, 2, clusters)
    cells = everyone[:, 3 * STENCIL + 2].astype(jnp.int32)[:, None, None, None, :]
    cells = cells + lax.broadcasted_iota(jnp.int32, shape, 1)
    turns = cells * third_bins[:, None, None] + lax.broadcasted_iota(jnp.int32, shape, 3) * (G // 4)
    phases = jnp.cos((turns % G).astype(f32) * (2.0 * math.pi / G)) * live[:, None, None]
    phases = phases.reshape(devices, SIDE, 2 * bins, clusters)

    tables = half_tables()
    tx = jnp.asarray(tables)
    txt = jnp.asarray(np.ascontiguousarray(np.swapaxes(tables, 2, 3)))
    if pars == 2:
        ty, tyt = tx, txt
    else:
        ty = lax.dynamic_slice_in_dim(tx, first_parity, 1, axis=0)
        tyt = lax.dynamic_slice_in_dim(txt, first_parity, 1, axis=0)

    whole_row = pl.BlockSpec((cols_total, height, clusters), lambda r: (r, 0, 0))
    phase_row = pl.BlockSpec((cols_total, SIDE, 2 * bins, clusters), lambda r: (r, 0, 0, 0))
    slab_block = pl.BlockSpec((parts, slab, G), lambda r: (0, r, 0))
    lanes = cols_total * SIDE * clusters
    field = pl.pallas_call(
        lambda *refs: scatter_kernel(cols_total, *refs),
        grid=(rows_total,),
        in_specs=[whole_row, phase_row],
        out_specs=slab_block,
        out_shape=jax.ShapeDtypeStruct((parts, G, G), f32),
        scratch_shapes=[
            pltpu.VMEM((slab, 2 * parts, lanes), bf16),
            pltpu.VMEM((G, lanes), bf16),
            pltpu.VMEM((2, slab * 2 * parts, HALF), f32),
        ],
        name="scatter",
    )(everyone, phases)

    plane = pl.BlockSpec((3, 1, 2, G, G), lambda m: (0, m, 0, 0, 0))
    smem = pl.BlockSpec(memory_space=pltpu.SMEM)
    table = pl.BlockSpec((2, 2, G, G), lambda m: (0, 0, 0, 0))
    table_y = pl.BlockSpec((pars, 2, G, G), lambda m: (0, 0, 0, 0))
    field = pl.pallas_call(
        dft_kernel,
        grid=(bins,),
        in_specs=[smem, smem, plane, table, table, table_y, table_y],
        out_specs=plane,
        out_shape=jax.ShapeDtypeStruct((3, bins, 2, G, G), f32),
        scratch_shapes=[
            pltpu.VMEM((3, 2, G, width), f32),
            pltpu.VMEM((3, 2, G, width), f32),
            pltpu.VMEM((3 * G, G), bf16),
            pltpu.VMEM((3 * G, G), bf16),
        ],
        name="spectral",
    )(signs, thirds, field.reshape(3, bins, 2, G, G), tx, txt, ty, tyt)

    sampled = pl.pallas_call(
        lambda *refs: gather_kernel(cols_total, *refs),
        grid=(rows_total,),
        in_specs=[whole_row, phase_row, slab_block],
        out_specs=pl.BlockSpec((cols_total, 3 * STENCIL, clusters), lambda r: (r, 0, 0)),
        out_shape=jax.ShapeDtypeStruct((devices, 3 * STENCIL, clusters), f32),
        scratch_shapes=[
            pltpu.VMEM((2, slab * parts, HALF), f32),
            pltpu.VMEM((slab * parts, SIDE * clusters), f32),
        ],
        name="gather",
    )(everyone, phases, field.reshape(parts, G, G))
    sampled = lax.all_to_all(sampled, AXES, 0, 0, tiled=True)
    sampled = jnp.sum(sampled, axis=0).reshape(3, STENCIL, clusters)
    far_term = jnp.einsum("csk,skp->ckp", sampled, weights_out, precision=precise)
    near_term = near_field(charges, near_tiles, pair_target, pair_landing, pair_count)
    return (far_term + near_term).reshape(3, -1)


def solution(mesh):
    in_specs = (
        P(None, AXES),
        P(None, AXES),
        P(None, AXES),
        P(None, AXES),
        P(AXES, None, None, None, None),
        P(AXES),
        P(AXES),
        P(AXES),
    )
    return jax.shard_map(
        per_device, mesh=mesh, in_specs=in_specs, out_specs=P(None, AXES), check_vma=False
    )
```

```python
import math

import jax
import jax.numpy as jnp
import numpy as np
from jax import lax
from jax.experimental import pallas as pl
from jax.experimental.pallas import tpu as pltpu
from jax.sharding import PartitionSpec as P

G = 256
HALF = G // 2
STENCIL = 27
SIDE = 3
AXES = ("row", "half", "core")
PEERS = ("row", "half")

precise = lax.Precision.HIGHEST
screen_shift = 0.5


def padded(cells, sides, width):
    for axis, dim in sides:
        count = lax.axis_size(axis)
        head = lax.slice_in_dim(cells, 0, width, axis=dim)
        tail = lax.slice_in_dim(cells, cells.shape[dim] - width, cells.shape[dim], axis=dim)
        cells = jnp.concatenate(
            [
                lax.ppermute(tail, axis, [(i, (i + 1) % count) for i in range(count)]),
                cells,
                lax.ppermute(head, axis, [((i + 1) % count, i) for i in range(count)]),
            ],
            axis=dim,
        )
    return cells


def near_field(charges, near_tiles, pair_target, pair_landing, pair_count):
    clusters, panels = charges.shape[1:]
    rounded = charges.astype(jnp.bfloat16)
    slot_total = pair_target.shape[0]
    slot_group = slot_total // 3
    picked = rounded[:, pair_target, :]
    partial_value = jnp.einsum(
        "qabij,aqi->qbj", near_tiles, picked, preferred_element_type=jnp.float32
    )
    live_mask = jnp.arange(slot_total, dtype=jnp.int32) < pair_count[0]
    partial_value = jnp.where(
        live_mask[:, None, None], partial_value, jnp.zeros_like(partial_value)
    )
    leaving = partial_value[slot_group:].reshape(slot_group, 2, 3, panels)
    arrived = padded(leaving, (("row", 1),), 1)
    crossing = jnp.stack([arrived[:, 3], arrived[:, 0]], axis=1).reshape(2 * slot_group, 3, panels)
    incoming = jnp.concatenate([partial_value[:slot_group], crossing], axis=0)
    landing_hot = (pair_landing[:, None] == jnp.arange(clusters, dtype=jnp.int32)[None, :]).astype(
        jnp.float32
    )
    return jnp.einsum("qk,qbj->bkj", landing_hot, incoming, precision=precise)


def half_tables():
    cells = np.arange(HALF)
    parts = []
    for parity in range(2):
        product = cells[:, None] * (2 * cells[None, :] + parity) % G
        angles = product * (2.0 * np.pi / G)
        cosines, sines = np.cos(angles), np.sin(angles)
        table = np.block([[cosines, -sines], [sines, cosines]]).astype(np.float32)
        high = table.astype(jnp.bfloat16)
        low = (table - high.astype(np.float32)).astype(jnp.bfloat16)
        parts.append(np.stack([high, low]))
    return np.stack(parts)


def split(values):
    high = values.astype(jnp.bfloat16)
    low = (values - high.astype(jnp.float32)).astype(jnp.bfloat16)
    return high, low


def dot(left, right):
    return jnp.dot(left, right, preferred_element_type=jnp.float32)


def three_pass(left_high, left_low, right_high, right_low):
    return (
        dot(left_high, right_low) + dot(left_low, right_high) + dot(left_high, right_high)
    )


def ordered(core, mine, other, stencils):
    for j in range(mine.shape[0]):
        stencils[2 * j + core] = mine[j]
        stencils[2 * j + 1 - core] = other[j]


def scatter_kernel(live, where, mine, other, out, phases, stencils, spread, hot, total):
    parts, slab, _ = out.shape
    cols, _, clusters = stencils.shape
    corner = pl.program_id(0) * slab
    ordered(where[0], mine, other, stencils)
    bins = lax.broadcasted_iota(jnp.int32, phases.shape[2:], 0)
    waves = bins // 2 + where[1]
    quarter = bins % 2 * (G // 4) + HALF
    kept = bins < 2 * live

    def block(c, carry):
        first = stencils[c, 3 * STENCIL : 3 * STENCIL + 1, :] - corner.astype(jnp.float32)
        second = stencils[c, 3 * STENCIL + 1 : 3 * STENCIL + 2, :]
        rows = lax.broadcasted_iota(jnp.int32, (G, clusters), 0).astype(jnp.float32)
        first_wide = jnp.broadcast_to(first, (2 * parts, clusters)).astype(jnp.bfloat16)
        third = stencils[c, 3 * STENCIL + 2 : 3 * STENCIL + 3, :].astype(jnp.int32)
        for z in range(SIDE):
            turns = (((third + z) * waves + quarter) & (G - 1)) - HALF
            turned = jnp.cos(turns.astype(jnp.float32) * (2.0 * math.pi / G))
            phases[c, z] = jnp.where(kept, turned, 0.0)
        for y in range(SIDE):
            lanes = pl.ds(pl.multiple_of((c * SIDE + y) * clusters, clusters), clusters)
            hot[:, lanes] = jnp.where(rows == second + y, 1.0, 0.0).astype(jnp.bfloat16)
            tiles = []
            for x in range(SIDE):
                modes = []
                for a in range(3):
                    at = a * STENCIL + x * 9 + y * 3
                    modes.append(
                        sum(stencils[c, at + z : at + z + 1, :] * phases[c, z] for z in range(SIDE))
                    )
                modes = jnp.concatenate(modes, axis=0)
                low = modes - modes.astype(jnp.bfloat16).astype(jnp.float32)
                tiles.append(jnp.concatenate([modes, low], axis=0).astype(jnp.bfloat16))
            blank = jnp.zeros_like(tiles[0])
            for cell in range(slab):
                value = blank
                for x in range(SIDE):
                    value = jnp.where(
                        first_wide == jnp.asarray(cell - x, jnp.bfloat16), tiles[x], value
                    )
                spread[cell, :, lanes] = value
        return carry

    lax.fori_loop(0, cols, block, 0)
    result = lax.dot_general(
        spread[...].reshape(slab * 2 * parts, hot.shape[1]),
        hot[...],
        (((1,), (1,)), ((), ())),
        preferred_element_type=jnp.float32,
    )
    for side in range(2):
        total[side] = result[:, side * HALF : (side + 1) * HALF]
    for side in range(2):
        for v in range(parts):
            out[v, :, side * HALF : (side + 1) * HALF] = (
                total[side, pl.ds(v, slab, stride=2 * parts), :]
                + total[side, pl.ds(parts + v, slab, stride=2 * parts), :]
            )


def dft_kernel(signs, thirds, field, tx, txt, ty, tyt, out, lines, modes, high, low):
    pars = ty.shape[0]
    width = pars * HALF

    def stage(values, at):
        high[at], low[at] = split(values)

    for p in range(pars):
        for a in range(3):
            for part in range(2):
                stage(
                    field[a, 0, part, :, :HALF] + signs[p] * field[a, 0, part, :, HALF:],
                    (slice(a * G, (a + 1) * G), slice(part * HALF, (part + 1) * HALF)),
                )
        for a in range(3):
            rows = slice(a * G, (a + 1) * G)
            result = three_pass(high[rows], low[rows], ty[p, 0], ty[p, 1])
            for part in range(2):
                lines[a, part, :, p * HALF : (p + 1) * HALF] = result[
                    :, part * HALF : (part + 1) * HALF
                ]
    for a in range(3):
        for q in range(2):
            rows = slice((2 * a + q) % 3 * G, ((2 * a + q) % 3 + 1) * G)
            for part in range(2):
                top, bottom = lines[a, part, :HALF], lines[a, part, HALF:]
                at = rows.start + part * HALF
                stage(top - bottom if q else top + bottom, (slice(at, at + HALF), slice(0, width)))
            result = three_pass(txt[q, 0], txt[q, 1], high[rows, :width], low[rows, :width])
            for part in range(2):
                modes[a, part, q * HALF : (q + 1) * HALF] = result[
                    part * HALF : (part + 1) * HALF
                ]

    m = pl.program_id(0)
    kthird = thirds[0, m]
    scale = thirds[1, m]
    chunk = 16

    def project(i, carry):
        rows = pl.ds(pl.multiple_of(i * chunk, chunk), chunk)
        at = lax.broadcasted_iota(jnp.int32, (chunk, width), 0) + i * chunk
        bin_first = jnp.where(at < HALF, 2 * at, 2 * at - (G - 1))
        lane = lax.broadcasted_iota(jnp.int32, (chunk, width), 1)
        second = []
        for p in range(pars):
            odd = jnp.where(signs[p] < 0.0, 1, 0)
            second.append(2 * (lane[:, p * HALF : (p + 1) * HALF] - p * HALF) + odd)
        bin_second = jnp.concatenate(second, axis=1) if pars > 1 else second[0]
        kept = (bin_first != HALF) & (bin_second != HALF)
        kfirst = jnp.where(bin_first < HALF, bin_first, bin_first - G).astype(jnp.float32)
        ksecond = jnp.where(bin_second < HALF, bin_second, bin_second - G).astype(jnp.float32)
        squared = kfirst * kfirst + ksecond * ksecond + kthird * kthird
        weighting = jnp.where(kept, scale / (squared + screen_shift), 0.0)
        inverse = 1.0 / jnp.maximum(squared, 1.0)
        for part in range(2):
            u, v, w = (modes[a, part, rows, :] for a in range(3))
            inner = (kfirst * u + ksecond * v + kthird * w) * inverse
            lines[0, part, rows, :] = (u - kfirst * inner) * weighting
            lines[1, part, rows, :] = (v - ksecond * inner) * weighting
            lines[2, part, rows, :] = (w - kthird * inner) * weighting
        return carry

    lax.fori_loop(0, G // chunk, project, 0)

    for a in range(3):
        results = []
        for q in range(2):
            rows = slice((2 * a + q) % 3 * G, ((2 * a + q) % 3 + 1) * G)
            for part in range(2):
                at = rows.start + part * HALF
                stage(
                    lines[a, part, q * HALF : (q + 1) * HALF],
                    (slice(at, at + HALF), slice(0, width)),
                )
            results.append(
                three_pass(tx[q, 0], tx[q, 1], high[rows, :width], low[rows, :width])
            )
        for part in range(2):
            even, odd = (r[part * HALF : (part + 1) * HALF] for r in results)
            modes[a, part, :HALF] = even + odd
            modes[a, part, HALF:] = even - odd
    for a in range(3):
        near = far = None
        for p in range(pars):
            rows = slice((2 * a + p) % 3 * G, ((2 * a + p) % 3 + 1) * G)
            for part in range(2):
                stage(
                    modes[a, part, :, p * HALF : (p + 1) * HALF],
                    (rows, slice(part * HALF, (part + 1) * HALF)),
                )
            result = three_pass(high[rows], low[rows], tyt[p, 0], tyt[p, 1])
            near = result if near is None else near + result
            far = signs[p] * result if far is None else far + signs[p] * result
        for part in range(2):
            out[a, 0, part, :, :HALF] = near[:, part * HALF : (part + 1) * HALF]
            out[a, 0, part, :, HALF:] = far[:, part * HALF : (part + 1) * HALF]


def gather_kernel(where, mine, other, phases, field, out, stencils, lines, found):
    parts, slab, _ = field.shape
    cols, _, clusters = stencils.shape
    ordered(where[0], mine, other, stencils)
    bins = parts // 3
    span = G // cols
    corner = (pl.program_id(0) * slab).astype(jnp.float32)
    for v in range(parts):
        for side in range(2):
            lines[side, pl.ds(v, slab, stride=parts), :] = field[
                v, :, side * HALF : (side + 1) * HALF
            ]
    for c in range(cols):
        first = stencils[c, 3 * STENCIL : 3 * STENCIL + 1, :] - corner
        second = stencils[c, 3 * STENCIL + 1 : 3 * STENCIL + 2, :]
        rows = lax.broadcasted_iota(jnp.int32, (2 * span, clusters), 0)
        rows = (jnp.where(rows < span, rows, rows - span) + c * span).astype(jnp.float32)
        hot = jnp.concatenate(
            [jnp.where(rows == second + y, 1.0, 0.0) for y in range(SIDE)], axis=1
        ).astype(jnp.bfloat16)
        side, start = divmod(c * span, HALF)
        values = lines[side, :, start : start + span]
        high, low = split(values)
        found[...] = dot(jnp.concatenate([high, low], axis=1), hot)
        wide = jnp.broadcast_to(first, (parts, clusters))
        for y in range(SIDE):
            lanes = slice(y * clusters, (y + 1) * clusters)
            sums = [jnp.zeros((parts, clusters), jnp.float32) for _ in range(SIDE)]
            for cell in range(slab):
                value = found[cell * parts : (cell + 1) * parts, lanes]
                for x in range(SIDE):
                    if 0 <= cell - x <= slab - SIDE:
                        sums[x] = jnp.where(wide == (cell - x), value, sums[x])
            for x in range(SIDE):
                for a in range(3):
                    mode = sums[x][a * bins : (a + 1) * bins]
                    for z in range(SIDE):
                        at = a * STENCIL + x * 9 + y * 3 + z
                        out[(c + where[0]) % 2, c // 2, at : at + 1, :] = jnp.sum(
                            mode * phases[c, z], axis=0, keepdims=True
                        )


def per_device(
    density,
    interp_weight,
    proj_weight,
    stencil_corner,
    near_tiles,
    pair_target,
    pair_landing,
    pair_count,
):
    clusters = stencil_corner.shape[1]
    panels = density.shape[1] // clusters
    rows_total = lax.axis_size("row")
    halves = lax.axis_size("half")
    cols_total = halves * lax.axis_size("core")
    devices = rows_total * cols_total
    core = lax.axis_index("core")
    device = lax.axis_index("row") * cols_total + lax.axis_index("half") * 2 + core
    swap = [(0, 1), (1, 0)]
    slab = G // rows_total
    kept_bins = G // 2
    third_parts = min(devices, kept_bins)
    second_parts = devices // third_parts
    pars = 2 // second_parts
    third_live = kept_bins // third_parts
    bins = max(4, third_live)
    parts = 3 * 2 * bins
    width = pars * HALF
    f32, bf16 = jnp.float32, jnp.bfloat16

    charges = density.reshape(3, clusters, panels)
    weights_in = interp_weight.reshape(STENCIL, clusters, panels)
    weights_out = proj_weight.reshape(STENCIL, clusters, panels)
    spread = jnp.einsum("ckp,skp->csk", charges, weights_in, precision=precise)
    packed = jnp.concatenate(
        [spread.reshape(3 * STENCIL, clusters), stencil_corner.astype(f32)], axis=0
    )
    height = 3 * STENCIL + 3
    peers = devices // 2
    mine = lax.all_to_all(
        jnp.broadcast_to(packed[None], (peers, height, clusters)), PEERS, 0, 0, tiled=True
    )
    other = lax.ppermute(mine, "core", swap)

    step = jnp.arange(bins, dtype=jnp.int32)
    third_bins = (device // second_parts) * third_live + step
    live = (step < third_live).astype(f32)
    factor = 1.0 / math.sqrt(density.shape[1] * devices)
    fold = jnp.where(third_bins == 0, 1.0, 2.0).astype(f32)
    thirds = jnp.stack([third_bins.astype(f32), live * fold * factor])
    first_parity = device % second_parts
    signs = 1.0 - 2.0 * (first_parity + jnp.arange(pars, dtype=jnp.int32)).astype(f32)

    where = jnp.stack([core, (device // second_parts) * third_live]).astype(jnp.int32)

    tables = half_tables()
    tx = jnp.asarray(tables)
    txt = jnp.asarray(np.ascontiguousarray(np.swapaxes(tables, 2, 3)))
    if pars == 2:
        ty, tyt = tx, txt
    else:
        ty = lax.dynamic_slice_in_dim(tx, first_parity, 1, axis=0)
        tyt = lax.dynamic_slice_in_dim(txt, first_parity, 1, axis=0)

    smem = pl.BlockSpec(memory_space=pltpu.SMEM)
    peer_row = pl.BlockSpec((halves, height, clusters), lambda r: (r, 0, 0))
    phase_row = pl.BlockSpec((cols_total, SIDE, 2 * bins, clusters), lambda r: (r, 0, 0, 0))
    slab_block = pl.BlockSpec((parts, slab, G), lambda r: (0, r, 0))
    lanes = cols_total * SIDE * clusters
    field, phases = pl.pallas_call(
        lambda *refs: scatter_kernel(third_live, *refs),
        grid=(rows_total,),
        in_specs=[smem, peer_row, peer_row],
        out_specs=[slab_block, phase_row],
        out_shape=[
            jax.ShapeDtypeStruct((parts, G, G), f32),
            jax.ShapeDtypeStruct((devices, SIDE, 2 * bins, clusters), f32),
        ],
        scratch_shapes=[
            pltpu.VMEM((cols_total, height, clusters), f32),
            pltpu.VMEM((slab, 2 * parts, lanes), bf16),
            pltpu.VMEM((G, lanes), bf16),
            pltpu.VMEM((2, slab * 2 * parts, HALF), f32),
        ],
        name="scatter",
    )(where, mine, other)

    plane = pl.BlockSpec((3, 1, 2, G, G), lambda m: (0, m, 0, 0, 0))
    table = pl.BlockSpec((2, 2, G, G), lambda m: (0, 0, 0, 0))
    table_y = pl.BlockSpec((pars, 2, G, G), lambda m: (0, 0, 0, 0))
    field = pl.pallas_call(
        dft_kernel,
        grid=(bins,),
        in_specs=[smem, smem, plane, table, table, table_y, table_y],
        out_specs=plane,
        out_shape=jax.ShapeDtypeStruct((3, bins, 2, G, G), f32),
        scratch_shapes=[
            pltpu.VMEM((3, 2, G, width), f32),
            pltpu.VMEM((3, 2, G, width), f32),
            pltpu.VMEM((3 * G, G), bf16),
            pltpu.VMEM((3 * G, G), bf16),
        ],
        name="spectral",
    )(signs, thirds, field.reshape(3, bins, 2, G, G), tx, txt, ty, tyt)

    sampled = pl.pallas_call(
        gather_kernel,
        grid=(rows_total,),
        in_specs=[smem, peer_row, peer_row, phase_row, slab_block],
        out_specs=pl.BlockSpec((2, halves, 3 * STENCIL, clusters), lambda r: (0, r, 0, 0)),
        out_shape=jax.ShapeDtypeStruct((2, peers, 3 * STENCIL, clusters), f32),
        scratch_shapes=[
            pltpu.VMEM((cols_total, height, clusters), f32),
            pltpu.VMEM((2, slab * parts, HALF), f32),
            pltpu.VMEM((slab * parts, SIDE * clusters), f32),
        ],
        name="gather",
    )(where, mine, other, phases, field.reshape(parts, G, G))
    sampled = sampled[0] + lax.ppermute(sampled[1], "core", swap)
    sampled = lax.all_to_all(sampled, PEERS, 0, 0, tiled=True)
    sampled = jnp.sum(sampled, axis=0).reshape(3, STENCIL, clusters)
    far_term = jnp.einsum("csk,skp->ckp", sampled, weights_out, precision=precise)
    near_term = near_field(charges, near_tiles, pair_target, pair_landing, pair_count)
    return (far_term + near_term).reshape(3, -1)


def solution(mesh):
    in_specs = (
        P(None, AXES),
        P(None, AXES),
        P(None, AXES),
        P(None, AXES),
        P(AXES, None, None, None, None),
        P(AXES),
        P(AXES),
        P(AXES),
    )
    rows_total, cols_total = (mesh.shape[axis] for axis in ("row", "col"))
    split_mesh = jax.sharding.Mesh(mesh.devices.reshape(rows_total, cols_total // 2, 2), AXES)
    return jax.shard_map(
        per_device, mesh=split_mesh, in_specs=in_specs, out_specs=P(None, AXES), check_vma=False
    )
```

```python
import math

import jax
import jax.numpy as jnp
import numpy as np
from jax import lax
from jax.experimental import pallas as pl
from jax.experimental.pallas import tpu as pltpu
from jax.sharding import PartitionSpec as P

G = 256
HALF = G // 2
STENCIL = 27
SIDE = 3
FINE = 4
AXES = ("row", "half", "core")
PEERS = ("row", "half")

precise = lax.Precision.HIGHEST
screen_shift = 0.5


def padded(cells, sides, width):
    for axis, dim in sides:
        count = lax.axis_size(axis)
        head = lax.slice_in_dim(cells, 0, width, axis=dim)
        tail = lax.slice_in_dim(cells, cells.shape[dim] - width, cells.shape[dim], axis=dim)
        cells = jnp.concatenate(
            [
                lax.ppermute(tail, axis, [(i, (i + 1) % count) for i in range(count)]),
                cells,
                lax.ppermute(head, axis, [((i + 1) % count, i) for i in range(count)]),
            ],
            axis=dim,
        )
    return cells


def near_field(charges, near_tiles, pair_target, pair_landing, pair_count):
    clusters, panels = charges.shape[1:]
    rounded = charges.astype(jnp.bfloat16)
    slot_total = pair_target.shape[0]
    slot_group = slot_total // 3
    picked = rounded[:, pair_target, :]
    partial_value = jnp.einsum(
        "qabij,aqi->qbj", near_tiles, picked, preferred_element_type=jnp.float32
    )
    live_mask = jnp.arange(slot_total, dtype=jnp.int32) < pair_count[0]
    partial_value = jnp.where(
        live_mask[:, None, None], partial_value, jnp.zeros_like(partial_value)
    )
    leaving = partial_value[slot_group:].reshape(slot_group, 2, 3, panels)
    arrived = padded(leaving, (("row", 1),), 1)
    crossing = jnp.stack([arrived[:, 3], arrived[:, 0]], axis=1).reshape(2 * slot_group, 3, panels)
    incoming = jnp.concatenate([partial_value[:slot_group], crossing], axis=0)
    landing_hot = (pair_landing[:, None] == jnp.arange(clusters, dtype=jnp.int32)[None, :]).astype(
        jnp.float32
    )
    return jnp.einsum("qk,qbj->bkj", landing_hot, incoming, precision=precise)


def half_tables():
    cells = np.arange(HALF)
    parts = []
    for parity in range(2):
        product = cells[:, None] * (2 * cells[None, :] + parity) % G
        angles = product * (2.0 * np.pi / G)
        cosines, sines = np.cos(angles), np.sin(angles)
        table = np.block([[cosines, -sines], [sines, cosines]]).astype(np.float32)
        high = table.astype(jnp.bfloat16)
        low = (table - high.astype(np.float32)).astype(jnp.bfloat16)
        parts.append(np.stack([high, low]))
    return np.stack(parts)


def split(values):
    high = values.astype(jnp.bfloat16)
    low = (values - high.astype(jnp.float32)).astype(jnp.bfloat16)
    return high, low


def dot(left, right):
    return jnp.dot(left, right, preferred_element_type=jnp.float32)


def three_pass(left_high, left_low, right_high, right_low):
    return (
        dot(left_high, right_low) + dot(left_low, right_high) + dot(left_high, right_high)
    )


def ordered(core, mine, other, stencils):
    for j in range(mine.shape[0]):
        stencils[2 * j + core] = mine[j]
        stencils[2 * j + 1 - core] = other[j]


def cosine(turns):
    turns = turns & (G - 1)
    turns = jnp.minimum(turns, G - turns)
    flipped = turns > G // 4
    angle = jnp.where(flipped, G // 2 - turns, turns).astype(jnp.float32) * (2.0 * math.pi / G)
    square = angle * angle
    total = jnp.full_like(square, 1.0 / math.factorial(12))
    for order in (10, 8, 6, 4, 2, 0):
        total = total * square + (-1.0) ** (order // 2) / math.factorial(order)
    return jnp.where(flipped, -total, total)


def scatter_kernel(live, where, mine, other, out, phases, stencils, spread, hot, total):
    sides, parts, slab, lanes = out.shape
    cols, _, clusters = stencils.shape
    span = G // cols
    high_cells = slab // FINE
    corner = pl.program_id(0) * slab
    ordered(where[0], mine, other, stencils)
    bins = lax.broadcasted_iota(jnp.int32, phases.shape[2:], 0)
    waves = bins // 2 + where[1]
    quarter = bins % 2 * (G // 4)
    kept = bins < 2 * live
    bf16 = jnp.bfloat16
    columns = lax.broadcasted_iota(jnp.int32, (FINE * span, clusters), 0)
    columns = columns.astype(jnp.float32).astype(bf16)
    for c in range(cols):
        first, second, third = (
            stencils[c, 3 * STENCIL + i : 3 * STENCIL + i + 1, :].astype(jnp.int32)
            for i in range(3)
        )
        for z in range(SIDE):
            phases[c, z] = jnp.where(kept, cosine((third + z) * waves + quarter), 0.0)
        for x in range(SIDE):
            cell = first - corner + x
            fine = (cell & (FINE - 1)) * span + second - c * span
            coarse = (cell // FINE).astype(jnp.float32)
            coarse = jnp.broadcast_to(coarse, (2 * parts, clusters)).astype(bf16)
            for y in range(SIDE):
                at = slice((x * SIDE + y) * clusters, (x * SIDE + y + 1) * clusters)
                target = jnp.broadcast_to((fine + y).astype(jnp.float32), columns.shape)
                hot[c, :, at] = jnp.where(
                    columns == target.astype(bf16), jnp.ones_like(columns), jnp.zeros_like(columns)
                )
                modes = []
                for a in range(3):
                    row = a * STENCIL + x * 9 + y * 3
                    modes.append(
                        sum(
                            stencils[c, row + z : row + z + 1, :] * phases[c, z]
                            for z in range(SIDE)
                        )
                    )
                modes = jnp.concatenate(modes, axis=0)
                low = modes - modes.astype(bf16).astype(jnp.float32)
                tile = jnp.concatenate([modes, low], axis=0).astype(bf16)
                for h in range(high_cells):
                    spread[c, h, :, at] = jnp.where(
                        coarse == jnp.asarray(h, bf16), tile, jnp.zeros_like(tile)
                    )
        result = lax.dot_general(
            spread[c].reshape(high_cells * 2 * parts, SIDE * SIDE * clusters),
            hot[c],
            (((1,), (1,)), ((), ())),
            preferred_element_type=jnp.float32,
        )
        for part in range(total.shape[1]):
            total[c, part] = result[:, part * lanes : (part + 1) * lanes]
    across = lanes // span
    for side in range(sides):
        for fine in range(FINE):
            part, start = divmod(fine * span, lanes)
            for v in range(parts):
                pieces = []
                for c in range(side * across, (side + 1) * across):
                    piece = (
                        total[c, part, pl.ds(v, high_cells, stride=2 * parts), :]
                        + total[c, part, pl.ds(parts + v, high_cells, stride=2 * parts), :]
                    )
                    pieces.append(piece[:, start : start + span])
                out[side, v, pl.ds(fine, high_cells, stride=FINE), :] = jnp.concatenate(
                    pieces, axis=1
                )


def dft_kernel(signs, thirds, field, tx, txt, ty, tyt, out, lines, modes, high, low):
    pars = ty.shape[0]
    width = pars * HALF

    def stage(values, at):
        high[at], low[at] = split(values)

    for p in range(pars):
        for a in range(3):
            for part in range(2):
                stage(
                    field[0, a, 0, part] + signs[p] * field[1, a, 0, part],
                    (slice(a * G, (a + 1) * G), slice(part * HALF, (part + 1) * HALF)),
                )
        for a in range(3):
            rows = slice(a * G, (a + 1) * G)
            result = three_pass(high[rows], low[rows], ty[p, 0], ty[p, 1])
            for part in range(2):
                lines[a, part, :, p * HALF : (p + 1) * HALF] = result[
                    :, part * HALF : (part + 1) * HALF
                ]
    for a in range(3):
        for q in range(2):
            rows = slice((2 * a + q) % 3 * G, ((2 * a + q) % 3 + 1) * G)
            for part in range(2):
                top, bottom = lines[a, part, :HALF], lines[a, part, HALF:]
                at = rows.start + part * HALF
                stage(top - bottom if q else top + bottom, (slice(at, at + HALF), slice(0, width)))
            result = three_pass(txt[q, 0], txt[q, 1], high[rows, :width], low[rows, :width])
            for part in range(2):
                modes[a, part, q * HALF : (q + 1) * HALF] = result[
                    part * HALF : (part + 1) * HALF
                ]

    m = pl.program_id(0)
    kthird = thirds[0, m]
    scale = thirds[1, m]
    chunk = 16

    def project(i, carry):
        rows = pl.ds(pl.multiple_of(i * chunk, chunk), chunk)
        at = lax.broadcasted_iota(jnp.int32, (chunk, width), 0) + i * chunk
        bin_first = jnp.where(at < HALF, 2 * at, 2 * at - (G - 1))
        lane = lax.broadcasted_iota(jnp.int32, (chunk, width), 1)
        second = []
        for p in range(pars):
            odd = jnp.where(signs[p] < 0.0, 1, 0)
            second.append(2 * (lane[:, p * HALF : (p + 1) * HALF] - p * HALF) + odd)
        bin_second = jnp.concatenate(second, axis=1) if pars > 1 else second[0]
        kept = (bin_first != HALF) & (bin_second != HALF)
        kfirst = jnp.where(bin_first < HALF, bin_first, bin_first - G).astype(jnp.float32)
        ksecond = jnp.where(bin_second < HALF, bin_second, bin_second - G).astype(jnp.float32)
        squared = kfirst * kfirst + ksecond * ksecond + kthird * kthird
        weighting = jnp.where(kept, scale / (squared + screen_shift), 0.0)
        inverse = 1.0 / jnp.maximum(squared, 1.0)
        for part in range(2):
            u, v, w = (modes[a, part, rows, :] for a in range(3))
            inner = (kfirst * u + ksecond * v + kthird * w) * inverse
            lines[0, part, rows, :] = (u - kfirst * inner) * weighting
            lines[1, part, rows, :] = (v - ksecond * inner) * weighting
            lines[2, part, rows, :] = (w - kthird * inner) * weighting
        return carry

    lax.fori_loop(0, G // chunk, project, 0)

    for a in range(3):
        results = []
        for q in range(2):
            rows = slice((2 * a + q) % 3 * G, ((2 * a + q) % 3 + 1) * G)
            for part in range(2):
                at = rows.start + part * HALF
                stage(
                    lines[a, part, q * HALF : (q + 1) * HALF],
                    (slice(at, at + HALF), slice(0, width)),
                )
            results.append(
                three_pass(tx[q, 0], tx[q, 1], high[rows, :width], low[rows, :width])
            )
        for part in range(2):
            even, odd = (r[part * HALF : (part + 1) * HALF] for r in results)
            modes[a, part, :HALF] = even + odd
            modes[a, part, HALF:] = even - odd
    for a in range(3):
        near = far = None
        for p in range(pars):
            rows = slice((2 * a + p) % 3 * G, ((2 * a + p) % 3 + 1) * G)
            for part in range(2):
                stage(
                    modes[a, part, :, p * HALF : (p + 1) * HALF],
                    (rows, slice(part * HALF, (part + 1) * HALF)),
                )
            result = three_pass(high[rows], low[rows], tyt[p, 0], tyt[p, 1])
            near = result if near is None else near + result
            far = signs[p] * result if far is None else far + signs[p] * result
        for part in range(2):
            out[0, a, 0, part] = near[:, part * HALF : (part + 1) * HALF]
            out[1, a, 0, part] = far[:, part * HALF : (part + 1) * HALF]


def gather_kernel(where, mine, other, phases, field, out, stencils, lines, found):
    _, parts, slab, _ = field.shape
    cols, _, clusters = stencils.shape
    ordered(where[0], mine, other, stencils)
    bins = parts // 3
    span = G // cols
    corner = (pl.program_id(0) * slab).astype(jnp.float32)
    for v in range(parts):
        for side in range(2):
            lines[side, pl.ds(v, slab, stride=parts), :] = field[side, v]
    for c in range(cols):
        first = stencils[c, 3 * STENCIL : 3 * STENCIL + 1, :] - corner
        second = stencils[c, 3 * STENCIL + 1 : 3 * STENCIL + 2, :]
        rows = lax.broadcasted_iota(jnp.int32, (2 * span, clusters), 0)
        rows = (jnp.where(rows < span, rows, rows - span) + c * span).astype(jnp.float32)
        hot = jnp.concatenate(
            [jnp.where(rows == second + y, 1.0, 0.0) for y in range(SIDE)], axis=1
        ).astype(jnp.bfloat16)
        side, start = divmod(c * span, HALF)
        values = lines[side, :, start : start + span]
        high, low = split(values)
        found[...] = dot(jnp.concatenate([high, low], axis=1), hot)
        wide = jnp.broadcast_to(first, (parts, clusters))
        for y in range(SIDE):
            lanes = slice(y * clusters, (y + 1) * clusters)
            sums = [jnp.zeros((parts, clusters), jnp.float32) for _ in range(SIDE)]
            for cell in range(slab):
                value = found[cell * parts : (cell + 1) * parts, lanes]
                for x in range(SIDE):
                    if 0 <= cell - x <= slab - SIDE:
                        sums[x] = jnp.where(wide == (cell - x), value, sums[x])
            for x in range(SIDE):
                for a in range(3):
                    mode = sums[x][a * bins : (a + 1) * bins]
                    for z in range(SIDE):
                        at = a * STENCIL + x * 9 + y * 3 + z
                        out[(c + where[0]) % 2, c // 2, at : at + 1, :] = jnp.sum(
                            mode * phases[c, z], axis=0, keepdims=True
                        )


def per_device(
    density,
    interp_weight,
    proj_weight,
    stencil_corner,
    near_tiles,
    pair_target,
    pair_landing,
    pair_count,
):
    clusters = stencil_corner.shape[1]
    panels = density.shape[1] // clusters
    rows_total = lax.axis_size("row")
    halves = lax.axis_size("half")
    cols_total = halves * lax.axis_size("core")
    devices = rows_total * cols_total
    core = lax.axis_index("core")
    device = lax.axis_index("row") * cols_total + lax.axis_index("half") * 2 + core
    swap = [(0, 1), (1, 0)]
    slab = G // rows_total
    kept_bins = G // 2
    third_parts = min(devices, kept_bins)
    second_parts = devices // third_parts
    pars = 2 // second_parts
    third_live = kept_bins // third_parts
    bins = max(4, third_live)
    parts = 3 * 2 * bins
    width = pars * HALF
    f32, bf16 = jnp.float32, jnp.bfloat16

    charges = density.reshape(3, clusters, panels)
    weights_in = interp_weight.reshape(STENCIL, clusters, panels)
    weights_out = proj_weight.reshape(STENCIL, clusters, panels)
    spread = jnp.einsum("ckp,skp->csk", charges, weights_in, precision=precise)
    packed = jnp.concatenate(
        [spread.reshape(3 * STENCIL, clusters), stencil_corner.astype(f32)], axis=0
    )
    height = 3 * STENCIL + 3
    peers = devices // 2
    mine = lax.all_to_all(
        jnp.broadcast_to(packed[None], (peers, height, clusters)), PEERS, 0, 0, tiled=True
    )
    other = lax.ppermute(mine, "core", swap)

    step = jnp.arange(bins, dtype=jnp.int32)
    third_bins = (device // second_parts) * third_live + step
    live = (step < third_live).astype(f32)
    factor = 1.0 / math.sqrt(density.shape[1] * devices)
    fold = jnp.where(third_bins == 0, 1.0, 2.0).astype(f32)
    thirds = jnp.stack([third_bins.astype(f32), live * fold * factor])
    first_parity = device % second_parts
    signs = 1.0 - 2.0 * (first_parity + jnp.arange(pars, dtype=jnp.int32)).astype(f32)

    where = jnp.stack([core, (device // second_parts) * third_live]).astype(jnp.int32)

    tables = half_tables()
    tx = jnp.asarray(tables)
    txt = jnp.asarray(np.ascontiguousarray(np.swapaxes(tables, 2, 3)))
    if pars == 2:
        ty, tyt = tx, txt
    else:
        ty = lax.dynamic_slice_in_dim(tx, first_parity, 1, axis=0)
        tyt = lax.dynamic_slice_in_dim(txt, first_parity, 1, axis=0)

    smem = pl.BlockSpec(memory_space=pltpu.SMEM)
    peer_row = pl.BlockSpec((halves, height, clusters), lambda r: (r, 0, 0))
    phase_row = pl.BlockSpec((cols_total, SIDE, 2 * bins, clusters), lambda r: (r, 0, 0, 0))
    slab_block = pl.BlockSpec((2, parts, slab, HALF), lambda r: (0, 0, r, 0))
    span = G // cols_total
    field, phases = pl.pallas_call(
        lambda *refs: scatter_kernel(third_live, *refs),
        grid=(rows_total,),
        in_specs=[smem, peer_row, peer_row],
        out_specs=[slab_block, phase_row],
        out_shape=[
            jax.ShapeDtypeStruct((2, parts, G, HALF), f32),
            jax.ShapeDtypeStruct((devices, SIDE, 2 * bins, clusters), f32),
        ],
        scratch_shapes=[
            pltpu.VMEM((cols_total, height, clusters), f32),
            pltpu.VMEM((cols_total, slab // FINE, 2 * parts, SIDE * SIDE * clusters), bf16),
            pltpu.VMEM((cols_total, FINE * span, SIDE * SIDE * clusters), bf16),
            pltpu.VMEM((cols_total, FINE * span // HALF, slab // FINE * 2 * parts, HALF), f32),
        ],
        name="scatter",
    )(where, mine, other)

    plane = pl.BlockSpec((2, 3, 1, 2, G, HALF), lambda m: (0, 0, m, 0, 0, 0))
    table = pl.BlockSpec((2, 2, G, G), lambda m: (0, 0, 0, 0))
    table_y = pl.BlockSpec((pars, 2, G, G), lambda m: (0, 0, 0, 0))
    field = pl.pallas_call(
        dft_kernel,
        grid=(bins,),
        in_specs=[smem, smem, plane, table, table, table_y, table_y],
        out_specs=plane,
        out_shape=jax.ShapeDtypeStruct((2, 3, bins, 2, G, HALF), f32),
        scratch_shapes=[
            pltpu.VMEM((3, 2, G, width), f32),
            pltpu.VMEM((3, 2, G, width), f32),
            pltpu.VMEM((3 * G, G), bf16),
            pltpu.VMEM((3 * G, G), bf16),
        ],
        name="spectral",
    )(signs, thirds, field.reshape(2, 3, bins, 2, G, HALF), tx, txt, ty, tyt)

    sampled = pl.pallas_call(
        gather_kernel,
        grid=(rows_total,),
        in_specs=[smem, peer_row, peer_row, phase_row, slab_block],
        out_specs=pl.BlockSpec((2, halves, 3 * STENCIL, clusters), lambda r: (0, r, 0, 0)),
        out_shape=jax.ShapeDtypeStruct((2, peers, 3 * STENCIL, clusters), f32),
        scratch_shapes=[
            pltpu.VMEM((cols_total, height, clusters), f32),
            pltpu.VMEM((2, slab * parts, HALF), f32),
            pltpu.VMEM((slab * parts, SIDE * clusters), f32),
        ],
        name="gather",
    )(where, mine, other, phases, field.reshape(2, parts, G, HALF))
    sampled = sampled[0] + lax.ppermute(sampled[1], "core", swap)
    sampled = lax.all_to_all(sampled, PEERS, 0, 0, tiled=True)
    sampled = jnp.sum(sampled, axis=0).reshape(3, STENCIL, clusters)
    far_term = jnp.einsum("csk,skp->ckp", sampled, weights_out, precision=precise)
    near_term = near_field(charges, near_tiles, pair_target, pair_landing, pair_count)
    return (far_term + near_term).reshape(3, -1)


def solution(mesh):
    in_specs = (
        P(None, AXES),
        P(None, AXES),
        P(None, AXES),
        P(None, AXES),
        P(AXES, None, None, None, None),
        P(AXES),
        P(AXES),
        P(AXES),
    )
    rows_total, cols_total = (mesh.shape[axis] for axis in ("row", "col"))
    split_mesh = jax.sharding.Mesh(mesh.devices.reshape(rows_total, cols_total // 2, 2), AXES)
    return jax.shard_map(
        per_device, mesh=split_mesh, in_specs=in_specs, out_specs=P(None, AXES), check_vma=False
    )
```

```python
import math

import jax
import jax.numpy as jnp
import numpy as np
from jax import lax
from jax.experimental import pallas as pl
from jax.experimental.pallas import tpu as pltpu
from jax.sharding import PartitionSpec as P

G = 256
HALF = G // 2
STENCIL = 27
SIDE = 3
FINE = 4
ROW = ("z", "x")
PLANE = ("x", "y")
AXES = ("z", "x", "y", "core")

screen_shift = 0.5


def swapped(values, axes, offset):
    count = lax.axis_size(axes)
    return lax.ppermute(values, axes, [(i, i ^ offset) for i in range(count)])


def row_shift(values, by):
    count = lax.axis_size(ROW)
    return lax.ppermute(values, ROW, [(i, (i + by) % count) for i in range(count)])


def near_field(charges, near_tiles, pair_target, pair_count):
    panels = charges.shape[2]
    rounded = charges.astype(jnp.bfloat16)
    slot_total = pair_target.shape[0]
    slot_group = slot_total // 3
    picked = rounded[:, pair_target, :]
    partial_value = jnp.einsum(
        "qabij,aqi->qbj", near_tiles, picked, preferred_element_type=jnp.float32
    )
    live_mask = jnp.arange(slot_total, dtype=jnp.int32) < pair_count[0]
    partial_value = jnp.where(
        live_mask[:, None, None], partial_value, jnp.zeros_like(partial_value)
    )
    leaving = partial_value[slot_group:].reshape(slot_group, 2, 3, panels)
    crossing = jnp.stack([row_shift(leaving[:, 0], -1), row_shift(leaving[:, 1], 1)], axis=1)
    return jnp.concatenate(
        [partial_value[:slot_group], crossing.reshape(2 * slot_group, 3, panels)], axis=0
    )


def half_tables():
    cells = np.arange(HALF)
    parts = []
    for parity in range(2):
        product = cells[:, None] * (2 * cells[None, :] + parity) % G
        angles = product * (2.0 * np.pi / G)
        cosines, sines = np.cos(angles), np.sin(angles)
        table = np.block([[cosines, -sines], [sines, cosines]]).astype(np.float32)
        high = table.astype(jnp.bfloat16)
        low = (table - high.astype(np.float32)).astype(jnp.bfloat16)
        parts.append(np.stack([high, low]))
    return np.stack(parts)


def split(values):
    high = values.astype(jnp.bfloat16)
    low = (values - high.astype(jnp.float32)).astype(jnp.bfloat16)
    return high, low


def dot(left, right):
    return jnp.dot(left, right, preferred_element_type=jnp.float32)


def three_pass(left_high, left_low, right_high, right_low):
    return (
        dot(left_high, right_low) + dot(left_low, right_high) + dot(left_high, right_high)
    )


def spread_kernel(density, weights, corners, out):
    clusters = corners.shape[1]
    panels = density.shape[1] // clusters
    unroll = 8
    lane = lax.broadcasted_iota(jnp.int32, (STENCIL, clusters), 1)

    def some(i, sums):
        for j in range(unroll):
            k = i * unroll + j
            at = pl.ds(pl.multiple_of(k * panels, panels), panels)
            weight = weights[:, at]
            sums = tuple(
                jnp.where(
                    lane == k,
                    jnp.sum(weight * density[a : a + 1, at], axis=1, keepdims=True),
                    sums[a],
                )
                for a in range(3)
            )
        return sums

    blank = jnp.zeros((STENCIL, clusters), jnp.float32)
    sums = lax.fori_loop(0, clusters // unroll, some, (blank, blank, blank))
    for a in range(3):
        out[a * STENCIL : (a + 1) * STENCIL, :] = sums[a]
    out[3 * STENCIL :, :] = corners[...].astype(jnp.float32)


def final_kernel(landing, near, weights, *refs):
    *samples, out = refs
    clusters = samples[0].shape[1]
    panels = weights.shape[1] // clusters
    total = sum(sample[...] for sample in samples[1:]) + samples[0][...]
    columns = [total[a * STENCIL : (a + 1) * STENCIL] for a in range(3)]
    for k in range(clusters):
        at = slice(k * panels, (k + 1) * panels)
        weight = weights[:, at]
        for a in range(3):
            out[a : a + 1, at] = jnp.sum(
                columns[a][:, k : k + 1] * weight, axis=0, keepdims=True
            )
    for q in range(near.shape[0]):
        at = pl.ds(pl.multiple_of(landing[q] * panels, panels), panels)
        out[:, at] = out[:, at] + near[q]


def ordered(where, mine, other, stencils):
    for j in range(mine.shape[1]):
        y = j ^ where[4]
        stencils[2 * y + where[0]] = mine[0, j, 0]
        stencils[2 * y + 1 - where[0]] = other[0, j, 0]


def cosine(turns):
    turns = turns & (G - 1)
    turns = jnp.minimum(turns, G - turns)
    flipped = turns > G // 4
    angle = jnp.where(flipped, G // 2 - turns, turns).astype(jnp.float32) * (2.0 * math.pi / G)
    square = angle * angle
    total = jnp.full_like(square, 1.0 / math.factorial(12))
    for order in (10, 8, 6, 4, 2, 0):
        total = total * square + (-1.0) ** (order // 2) / math.factorial(order)
    return jnp.where(flipped, -total, total)


def scatter_kernel(live, where, mine, other, out, phases, stencils, spread, hot, total):
    sides, parts, slab, lanes = out.shape
    cols, _, clusters = stencils.shape
    span = G // cols
    high_cells = slab // FINE
    corner = pl.program_id(0) * slab
    ordered(where, mine, other, stencils)
    bins = lax.broadcasted_iota(jnp.int32, phases.shape[2:], 0)
    waves = bins // 2 + where[1]
    quarter = bins % 2 * (G // 4)
    kept = bins < 2 * live
    bf16 = jnp.bfloat16
    columns = lax.broadcasted_iota(jnp.int32, (FINE * span, clusters), 0)
    columns = columns.astype(jnp.float32).astype(bf16)
    for c in range(cols):
        first, second, third = (
            stencils[c, 3 * STENCIL + i : 3 * STENCIL + i + 1, :].astype(jnp.int32)
            for i in range(3)
        )
        for z in range(SIDE):
            phases[c, z] = jnp.where(kept, cosine((third + z) * waves + quarter), 0.0)
        for x in range(SIDE):
            cell = first - corner + x
            fine = (cell & (FINE - 1)) * span + second - c * span
            coarse = (cell // FINE).astype(jnp.float32)
            coarse = jnp.broadcast_to(coarse, (2 * parts, clusters)).astype(bf16)
            for y in range(SIDE):
                at = slice((x * SIDE + y) * clusters, (x * SIDE + y + 1) * clusters)
                target = jnp.broadcast_to((fine + y).astype(jnp.float32), columns.shape)
                hot[c, :, at] = jnp.where(
                    columns == target.astype(bf16), jnp.ones_like(columns), jnp.zeros_like(columns)
                )
                modes = []
                for a in range(3):
                    row = a * STENCIL + x * 9 + y * 3
                    modes.append(
                        sum(
                            stencils[c, row + z : row + z + 1, :] * phases[c, z]
                            for z in range(SIDE)
                        )
                    )
                modes = jnp.concatenate(modes, axis=0)
                low = modes - modes.astype(bf16).astype(jnp.float32)
                tile = jnp.concatenate([modes, low], axis=0).astype(bf16)
                for h in range(high_cells):
                    spread[c, h, :, at] = jnp.where(
                        coarse == jnp.asarray(h, bf16), tile, jnp.zeros_like(tile)
                    )
        result = lax.dot_general(
            spread[c].reshape(high_cells * 2 * parts, SIDE * SIDE * clusters),
            hot[c],
            (((1,), (1,)), ((), ())),
            preferred_element_type=jnp.float32,
        )
        for part in range(total.shape[1]):
            total[c, part] = result[:, part * lanes : (part + 1) * lanes]
    across = lanes // span
    for side in range(sides):
        for fine in range(FINE):
            part, start = divmod(fine * span, lanes)
            for v in range(parts):
                pieces = []
                for c in range(side * across, (side + 1) * across):
                    piece = (
                        total[c, part, pl.ds(v, high_cells, stride=2 * parts), :]
                        + total[c, part, pl.ds(parts + v, high_cells, stride=2 * parts), :]
                    )
                    pieces.append(piece[:, start : start + span])
                out[side, v, pl.ds(fine, high_cells, stride=FINE), :] = jnp.concatenate(
                    pieces, axis=1
                )


def dft_kernel(signs, thirds, field, tx, txt, ty, tyt, out, lines, modes, high, low):
    pars = ty.shape[0]
    width = pars * HALF

    def stage(values, at):
        high[at], low[at] = split(values)

    for p in range(pars):
        for a in range(3):
            for part in range(2):
                stage(
                    field[0, a, 0, part] + signs[p] * field[1, a, 0, part],
                    (slice(a * G, (a + 1) * G), slice(part * HALF, (part + 1) * HALF)),
                )
        for a in range(3):
            rows = slice(a * G, (a + 1) * G)
            result = three_pass(high[rows], low[rows], ty[p, 0], ty[p, 1])
            for part in range(2):
                lines[a, part, :, p * HALF : (p + 1) * HALF] = result[
                    :, part * HALF : (part + 1) * HALF
                ]
    for a in range(3):
        for q in range(2):
            rows = slice((2 * a + q) % 3 * G, ((2 * a + q) % 3 + 1) * G)
            for part in range(2):
                top, bottom = lines[a, part, :HALF], lines[a, part, HALF:]
                at = rows.start + part * HALF
                stage(top - bottom if q else top + bottom, (slice(at, at + HALF), slice(0, width)))
            result = three_pass(txt[q, 0], txt[q, 1], high[rows, :width], low[rows, :width])
            for part in range(2):
                modes[a, part, q * HALF : (q + 1) * HALF] = result[
                    part * HALF : (part + 1) * HALF
                ]

    m = pl.program_id(0)
    kthird = thirds[0, m]
    scale = thirds[1, m]
    chunk = 16

    def project(i, carry):
        rows = pl.ds(pl.multiple_of(i * chunk, chunk), chunk)
        at = lax.broadcasted_iota(jnp.int32, (chunk, width), 0) + i * chunk
        bin_first = jnp.where(at < HALF, 2 * at, 2 * at - (G - 1))
        lane = lax.broadcasted_iota(jnp.int32, (chunk, width), 1)
        second = []
        for p in range(pars):
            odd = jnp.where(signs[p] < 0.0, 1, 0)
            second.append(2 * (lane[:, p * HALF : (p + 1) * HALF] - p * HALF) + odd)
        bin_second = jnp.concatenate(second, axis=1) if pars > 1 else second[0]
        kept = (bin_first != HALF) & (bin_second != HALF)
        kfirst = jnp.where(bin_first < HALF, bin_first, bin_first - G).astype(jnp.float32)
        ksecond = jnp.where(bin_second < HALF, bin_second, bin_second - G).astype(jnp.float32)
        squared = kfirst * kfirst + ksecond * ksecond + kthird * kthird
        weighting = jnp.where(kept, scale / (squared + screen_shift), 0.0)
        inverse = 1.0 / jnp.maximum(squared, 1.0)
        for part in range(2):
            u, v, w = (modes[a, part, rows, :] for a in range(3))
            inner = (kfirst * u + ksecond * v + kthird * w) * inverse
            lines[0, part, rows, :] = (u - kfirst * inner) * weighting
            lines[1, part, rows, :] = (v - ksecond * inner) * weighting
            lines[2, part, rows, :] = (w - kthird * inner) * weighting
        return carry

    lax.fori_loop(0, G // chunk, project, 0)

    for a in range(3):
        results = []
        for q in range(2):
            rows = slice((2 * a + q) % 3 * G, ((2 * a + q) % 3 + 1) * G)
            for part in range(2):
                at = rows.start + part * HALF
                stage(
                    lines[a, part, q * HALF : (q + 1) * HALF],
                    (slice(at, at + HALF), slice(0, width)),
                )
            results.append(
                three_pass(tx[q, 0], tx[q, 1], high[rows, :width], low[rows, :width])
            )
        for part in range(2):
            even, odd = (r[part * HALF : (part + 1) * HALF] for r in results)
            modes[a, part, :HALF] = even + odd
            modes[a, part, HALF:] = even - odd
    for a in range(3):
        near = far = None
        for p in range(pars):
            rows = slice((2 * a + p) % 3 * G, ((2 * a + p) % 3 + 1) * G)
            for part in range(2):
                stage(
                    modes[a, part, :, p * HALF : (p + 1) * HALF],
                    (rows, slice(part * HALF, (part + 1) * HALF)),
                )
            result = three_pass(high[rows], low[rows], tyt[p, 0], tyt[p, 1])
            near = result if near is None else near + result
            far = signs[p] * result if far is None else far + signs[p] * result
        for part in range(2):
            out[0, a, 0, part] = near[:, part * HALF : (part + 1) * HALF]
            out[1, a, 0, part] = far[:, part * HALF : (part + 1) * HALF]


def gather_kernel(where, mine, other, phases, field, out, stencils, lines, found):
    _, parts, slab, _ = field.shape
    cols, _, clusters = stencils.shape
    ordered(where, mine, other, stencils)
    bins = parts // 3
    span = G // cols
    corner = (pl.program_id(0) * slab).astype(jnp.float32)
    for v in range(parts):
        for side in range(2):
            lines[side, pl.ds(v, slab, stride=parts), :] = field[side, v]
    for c in range(cols):
        first = stencils[c, 3 * STENCIL : 3 * STENCIL + 1, :] - corner
        second = stencils[c, 3 * STENCIL + 1 : 3 * STENCIL + 2, :]
        rows = lax.broadcasted_iota(jnp.int32, (2 * span, clusters), 0)
        rows = (jnp.where(rows < span, rows, rows - span) + c * span).astype(jnp.float32)
        hot = jnp.concatenate(
            [jnp.where(rows == second + y, 1.0, 0.0) for y in range(SIDE)], axis=1
        ).astype(jnp.bfloat16)
        side, start = divmod(c * span, HALF)
        values = lines[side, :, start : start + span]
        high, low = split(values)
        found[...] = dot(jnp.concatenate([high, low], axis=1), hot)
        wide = jnp.broadcast_to(first, (parts, clusters))
        for y in range(SIDE):
            lanes = slice(y * clusters, (y + 1) * clusters)
            sums = [jnp.zeros((parts, clusters), jnp.float32) for _ in range(SIDE)]
            for cell in range(slab):
                value = found[cell * parts : (cell + 1) * parts, lanes]
                for x in range(SIDE):
                    if 0 <= cell - x <= slab - SIDE:
                        sums[x] = jnp.where(wide == (cell - x), value, sums[x])
            for x in range(SIDE):
                for a in range(3):
                    mode = sums[x][a * bins : (a + 1) * bins]
                    for z in range(SIDE):
                        at = a * STENCIL + x * 9 + y * 3 + z
                        out[(c + where[0]) % 2, 0, (c // 2) ^ where[4], 0, at : at + 1, :] = jnp.sum(
                            mode * phases[c, z], axis=0, keepdims=True
                        )


def per_device(
    density,
    interp_weight,
    proj_weight,
    stencil_corner,
    near_tiles,
    pair_target,
    pair_landing,
    pair_count,
):
    clusters = stencil_corner.shape[1]
    panels = density.shape[1] // clusters
    deep, wide, high = (lax.axis_size(axis) for axis in AXES[:3])
    here = [lax.axis_index(axis) for axis in AXES]
    rows_total = deep * wide
    cols_total = high * lax.axis_size("core")
    devices = rows_total * cols_total
    device = lax.axis_index(AXES)
    slab = G // rows_total
    kept_bins = G // 2
    third_parts = min(devices, kept_bins)
    second_parts = devices // third_parts
    pars = 2 // second_parts
    third_live = kept_bins // third_parts
    bins = max(4, third_live)
    parts = 3 * 2 * bins
    width = pars * HALF
    f32, bf16 = jnp.float32, jnp.bfloat16

    charges = density.reshape(3, clusters, panels)
    height = 3 * STENCIL + 3
    packed = pl.pallas_call(
        spread_kernel,
        out_shape=jax.ShapeDtypeStruct((height, clusters), f32),
        name="spread",
    )(density, interp_weight, stencil_corner)
    line = jnp.stack([packed] + [swapped(packed, "z", o) for o in range(1, deep)])
    mine = jnp.stack([line] + [swapped(line, PLANE, o) for o in range(1, wide * high)])
    mine = mine.reshape(wide, high, deep, height, clusters)
    other = swapped(mine, "core", 1)

    step = jnp.arange(bins, dtype=jnp.int32)
    third_bins = (device // second_parts) * third_live + step
    live = (step < third_live).astype(f32)
    factor = 1.0 / math.sqrt(density.shape[1] * devices)
    fold = jnp.where(third_bins == 0, 1.0, 2.0).astype(f32)
    thirds = jnp.stack([third_bins.astype(f32), live * fold * factor])
    first_parity = device % second_parts
    signs = 1.0 - 2.0 * (first_parity + jnp.arange(pars, dtype=jnp.int32)).astype(f32)

    where = jnp.stack([here[3], (device // second_parts) * third_live, here[0], here[1], here[2]])
    where = where.astype(jnp.int32)

    tables = half_tables()
    tx = jnp.asarray(tables)
    txt = jnp.asarray(np.ascontiguousarray(np.swapaxes(tables, 2, 3)))
    if pars == 2:
        ty, tyt = tx, txt
    else:
        ty = lax.dynamic_slice_in_dim(tx, first_parity, 1, axis=0)
        tyt = lax.dynamic_slice_in_dim(txt, first_parity, 1, axis=0)

    smem = pl.BlockSpec(memory_space=pltpu.SMEM)
    peer_row = pl.BlockSpec(
        (1, high, 1, height, clusters),
        lambda r, where: ((r % wide) ^ where[3], 0, (r // wide) ^ where[2], 0, 0),
    )
    phase_row = pl.BlockSpec(
        (cols_total, SIDE, 2 * bins, clusters), lambda r, where: (r, 0, 0, 0)
    )
    slab_block = pl.BlockSpec((2, parts, slab, HALF), lambda r, where: (0, 0, r, 0))
    span = G // cols_total
    field, phases = pl.pallas_call(
        lambda *refs: scatter_kernel(third_live, *refs),
        grid_spec=pltpu.PrefetchScalarGridSpec(
            num_scalar_prefetch=1,
            grid=(rows_total,),
            in_specs=[peer_row, peer_row],
            out_specs=[slab_block, phase_row],
            scratch_shapes=[
                pltpu.VMEM((cols_total, height, clusters), f32),
                pltpu.VMEM((cols_total, slab // FINE, 2 * parts, SIDE * SIDE * clusters), bf16),
                pltpu.VMEM((cols_total, FINE * span, SIDE * SIDE * clusters), bf16),
                pltpu.VMEM((cols_total, FINE * span // HALF, slab // FINE * 2 * parts, HALF), f32),
            ],
        ),
        out_shape=[
            jax.ShapeDtypeStruct((2, parts, G, HALF), f32),
            jax.ShapeDtypeStruct((devices, SIDE, 2 * bins, clusters), f32),
        ],
        name="scatter",
    )(where, mine, other)

    plane = pl.BlockSpec((2, 3, 1, 2, G, HALF), lambda m: (0, 0, m, 0, 0, 0))
    table = pl.BlockSpec((2, 2, G, G), lambda m: (0, 0, 0, 0))
    table_y = pl.BlockSpec((pars, 2, G, G), lambda m: (0, 0, 0, 0))
    field = pl.pallas_call(
        dft_kernel,
        grid=(bins,),
        in_specs=[smem, smem, plane, table, table, table_y, table_y],
        out_specs=plane,
        out_shape=jax.ShapeDtypeStruct((2, 3, bins, 2, G, HALF), f32),
        scratch_shapes=[
            pltpu.VMEM((3, 2, G, width), f32),
            pltpu.VMEM((3, 2, G, width), f32),
            pltpu.VMEM((3 * G, G), bf16),
            pltpu.VMEM((3 * G, G), bf16),
        ],
        name="spectral",
    )(signs, thirds, field.reshape(2, 3, bins, 2, G, HALF), tx, txt, ty, tyt)

    sampled = pl.pallas_call(
        gather_kernel,
        grid_spec=pltpu.PrefetchScalarGridSpec(
            num_scalar_prefetch=1,
            grid=(rows_total,),
            in_specs=[peer_row, peer_row, phase_row, slab_block],
            out_specs=pl.BlockSpec(
                (2, 1, high, 1, 3 * STENCIL, clusters),
                lambda r, where: (0, (r % wide) ^ where[3], 0, (r // wide) ^ where[2], 0, 0),
            ),
            scratch_shapes=[
                pltpu.VMEM((cols_total, height, clusters), f32),
                pltpu.VMEM((2, slab * parts, HALF), f32),
                pltpu.VMEM((slab * parts, SIDE * clusters), f32),
            ],
        ),
        out_shape=jax.ShapeDtypeStruct((2, wide, high, deep, 3 * STENCIL, clusters), f32),
        name="gather",
    )(where, mine, other, phases, field.reshape(2, parts, G, HALF))
    sampled = sampled.reshape(2, wide * high, deep, 3 * STENCIL, clusters)
    sampled = sampled[0] + swapped(sampled[1], "core", 1)
    line = sampled[0] + sum(swapped(sampled[o], PLANE, o) for o in range(1, wide * high))
    samples = [line[0]] + [swapped(line[o], "z", o) for o in range(1, deep)]
    near = near_field(
        density.reshape(3, clusters, panels), near_tiles, pair_target, pair_count
    )
    vmem = pl.BlockSpec(memory_space=pltpu.VMEM)
    return pl.pallas_call(
        final_kernel,
        in_specs=[smem] + [vmem] * (2 + deep),
        out_shape=jax.ShapeDtypeStruct(density.shape, f32),
        name="final",
    )(pair_landing, near, proj_weight, *samples)


def solution(mesh):
    in_specs = (
        P(None, AXES),
        P(None, AXES),
        P(None, AXES),
        P(None, AXES),
        P(AXES, None, None, None, None),
        P(AXES),
        P(AXES),
        P(AXES),
    )
    rows_total, cols_total = (mesh.shape[axis] for axis in ("row", "col"))
    high = cols_total // 2
    wide = high if rows_total % high == 0 else 1
    split_mesh = jax.sharding.Mesh(
        mesh.devices.reshape(rows_total // wide, wide, high, 2), AXES
    )
    return jax.shard_map(
        per_device, mesh=split_mesh, in_specs=in_specs, out_specs=P(None, AXES), check_vma=False
    )
```

```python
import functools
import math

import jax
import jax.numpy as jnp
import numpy as np
from jax import lax
from jax.experimental import pallas as pl
from jax.experimental.pallas import tpu as pltpu
from jax.sharding import PartitionSpec as P

G = 256
HALF = G // 2
STENCIL = 27
SIDE = 3
FINE = 4
SAMPLES = 3 * STENCIL
HEIGHT = 88
TILE = 16
ROW = ("z", "x")
PLANE = ("x", "y")
AXES = ("z", "x", "y", "core")

screen_shift = 0.5


def swapped(values, axes, offset):
    count = lax.axis_size(axes)
    return lax.ppermute(values, axes, [(i, i ^ offset) for i in range(count)])


def row_shift(values, by):
    count = lax.axis_size(ROW)
    return lax.ppermute(values, ROW, [(i, (i + by) % count) for i in range(count)])


def near_field(charges, near_tiles, pair_target, pair_count):
    panels = charges.shape[2]
    rounded = charges.astype(jnp.bfloat16)
    slot_total = pair_target.shape[0]
    slot_group = slot_total // 3
    picked = rounded[:, pair_target, :]
    partial_value = jnp.einsum(
        "qabij,aqi->qbj", near_tiles, picked, preferred_element_type=jnp.float32
    )
    live_mask = jnp.arange(slot_total, dtype=jnp.int32) < pair_count[0]
    partial_value = jnp.where(
        live_mask[:, None, None], partial_value, jnp.zeros_like(partial_value)
    )
    leaving = partial_value[slot_group:].reshape(slot_group, 2, 3, panels)
    crossing = jnp.stack([row_shift(leaving[:, 0], -1), row_shift(leaving[:, 1], 1)], axis=1)
    return jnp.concatenate(
        [partial_value[:slot_group], crossing.reshape(2 * slot_group, 3, panels)], axis=0
    )


def half_tables():
    cells = np.arange(HALF)
    parts = []
    for parity in range(2):
        product = cells[:, None] * (2 * cells[None, :] + parity) % G
        angles = product * (2.0 * np.pi / G)
        cosines, sines = np.cos(angles), np.sin(angles)
        table = np.block([[cosines, -sines], [sines, cosines]]).astype(np.float32)
        high = table.astype(jnp.bfloat16)
        low = (table - high.astype(np.float32)).astype(jnp.bfloat16)
        parts.append(np.stack([high, low]))
    return np.stack(parts)


def split(values):
    high = values.astype(jnp.bfloat16)
    low = (values - high.astype(jnp.float32)).astype(jnp.bfloat16)
    return high, low


def dot(left, right):
    return jnp.dot(left, right, preferred_element_type=jnp.float32)


def three_pass(left_high, left_low, right_high, right_low):
    return (
        dot(left_high, right_low) + dot(left_low, right_high) + dot(left_high, right_high)
    )


def spread_kernel(density, weights, corners, out):
    clusters = corners.shape[1]
    panels = density.shape[1] // clusters
    unroll = 8
    lane = lax.broadcasted_iota(jnp.int32, (STENCIL, clusters), 1)

    def some(i, sums):
        for j in range(unroll):
            k = i * unroll + j
            at = pl.ds(pl.multiple_of(k * panels, panels), panels)
            weight = weights[:, at]
            sums = tuple(
                jnp.where(
                    lane == k,
                    jnp.sum(weight * density[a : a + 1, at], axis=1, keepdims=True),
                    sums[a],
                )
                for a in range(3)
            )
        return sums

    blank = jnp.zeros((STENCIL, clusters), jnp.float32)
    sums = lax.fori_loop(0, clusters // unroll, some, (blank, blank, blank))
    for a in range(3):
        out[a * STENCIL : (a + 1) * STENCIL, :] = sums[a]
    out[SAMPLES : SAMPLES + 3, :] = corners[...].astype(jnp.float32)
    out[SAMPLES + 3 :, :] = jnp.zeros((HEIGHT - SAMPLES - 3, clusters), jnp.float32)


def final_kernel(landing, near, weights, *refs):
    *samples, out = refs
    clusters = samples[0].shape[1]
    panels = weights.shape[1] // clusters
    total = sum(sample[...] for sample in samples[1:]) + samples[0][...]
    columns = [total[a * STENCIL : (a + 1) * STENCIL] for a in range(3)]
    for k in range(clusters):
        at = slice(k * panels, (k + 1) * panels)
        weight = weights[:, at]
        for a in range(3):
            out[a : a + 1, at] = jnp.sum(
                columns[a][:, k : k + 1] * weight, axis=0, keepdims=True
            )
    for q in range(near.shape[0]):
        at = pl.ds(pl.multiple_of(landing[q] * panels, panels), panels)
        out[:, at] = out[:, at] + near[q]


def ordered(wide, high, where, sources, stencils):
    row = pl.program_id(0)
    deep = (row // wide) ^ where[2]
    for o in range(wide * high):

        @pl.when((row % wide) ^ where[3] == o // high)
        def _():
            y = (o % high) ^ where[4]
            stencils[2 * y + where[0]] = sources[o][deep]
            stencils[2 * y + 1 - where[0]] = sources[wide * high + o][deep]


def cosine(turns):
    turns = turns & (G - 1)
    turns = jnp.minimum(turns, G - turns)
    flipped = turns > G // 4
    angle = jnp.where(flipped, G // 2 - turns, turns).astype(jnp.float32) * (2.0 * math.pi / G)
    square = angle * angle
    total = jnp.full_like(square, 1.0 / math.factorial(12))
    for order in (10, 8, 6, 4, 2, 0):
        total = total * square + (-1.0) ** (order // 2) / math.factorial(order)
    return jnp.where(flipped, -total, total)


def regrouped(values, span, left):
    if len(values) == 2:
        turned = [pltpu.roll(value, span, axis=1) for value in values]
        return [
            jnp.where(left, values[0], turned[1]),
            jnp.where(left, turned[0], values[1]),
        ]
    return [
        jnp.concatenate([value[:, i * span : (i + 1) * span] for value in values], axis=1)
        for i in range(len(values))
    ]


def scatter_kernel(live, wide, high, where, *refs):
    *sources, out, phases, stencils, total = refs
    sides, parts, slab, lanes = out.shape
    cols, _, clusters = stencils.shape
    span = G // cols
    coarse_cells = slab // FINE
    corner = pl.program_id(0) * slab
    ordered(wide, high, where, sources, stencils)
    bins = lax.broadcasted_iota(jnp.int32, phases.shape[2:], 0)
    waves = bins // 2 + where[1]
    quarter = bins % 2 * (G // 4)
    kept = bins < 2 * live
    bf16 = jnp.bfloat16
    column = lax.broadcasted_iota(jnp.int32, (TILE, clusters), 0)
    ones = jnp.ones((TILE, clusters), bf16)
    zeros = jnp.zeros((TILE, clusters), bf16)
    for c in range(cols):
        first, second, third = (
            stencils[c, SAMPLES + i : SAMPLES + i + 1, :].astype(jnp.int32) for i in range(3)
        )
        for z in range(SIDE):
            phases[c, z] = jnp.where(kept, cosine((third + z) * waves + quarter), 0.0)
        hots, spreads = [], []
        for x in range(SIDE):
            cell = first - corner + x
            fine = (cell & (FINE - 1)) * span + second - c * span
            fine = jnp.broadcast_to(fine, (TILE, clusters))
            coarse = jnp.broadcast_to(cell // FINE, (TILE, clusters)).astype(jnp.int16)
            for y in range(SIDE):
                target = (fine + y).astype(jnp.int16)
                hots.append(
                    jnp.concatenate(
                        [
                            jnp.where((column + j).astype(jnp.int16) == target, ones, zeros)
                            for j in range(0, FINE * span, TILE)
                        ],
                        axis=0,
                    )
                )
                modes = []
                for a in range(3):
                    row = a * STENCIL + x * 9 + y * 3
                    modes.append(
                        sum(
                            stencils[c, row + z : row + z + 1, :] * phases[c, z]
                            for z in range(SIDE)
                        )
                    )
                modes = jnp.concatenate(modes, axis=0)
                low = modes - modes.astype(bf16).astype(jnp.float32)
                tile = jnp.concatenate([modes, low], axis=0).astype(bf16)
                pieces = []
                for h in range(coarse_cells):
                    chosen = coarse == jnp.asarray(h, jnp.int16)
                    for j in range(0, 2 * parts, TILE):
                        pieces.append(jnp.where(chosen, tile[j : j + TILE], zeros))
                spreads.append(jnp.concatenate(pieces, axis=0))
        result = lax.dot_general(
            jnp.concatenate(spreads, axis=1),
            jnp.concatenate(hots, axis=1),
            (((1,), (1,)), ((), ())),
            preferred_element_type=jnp.float32,
        )
        for part in range(total.shape[1]):
            total[c, part] = result[:, part * lanes : (part + 1) * lanes]
    across = lanes // span
    left = lax.broadcasted_iota(jnp.int32, (coarse_cells, lanes), 1) < span
    for part in range(total.shape[1]):
        for v in range(parts):
            for side in range(sides):
                values = [
                    total[c, part, pl.ds(v, coarse_cells, stride=2 * parts), :]
                    + total[c, part, pl.ds(parts + v, coarse_cells, stride=2 * parts), :]
                    for c in range(side * across, (side + 1) * across)
                ]
                for i, row in enumerate(regrouped(values, span, left)):
                    at = pl.ds(part * across + i, coarse_cells, stride=FINE)
                    out[side, v, at, :] = row


def dft_kernel(factor, live, where, field, tx, txt, ty, tyt, out, lines, modes):
    pars = ty.shape[0]
    width = pars * HALF
    odds = [where[5] + p for p in range(pars)]
    signs = [1.0 - 2.0 * odd.astype(jnp.float32) for odd in odds]

    for p in range(pars):
        for a in range(3):
            values = [field[0, a, 0, i] + signs[p] * field[1, a, 0, i] for i in range(2)]
            result = three_pass(*split(jnp.concatenate(values, axis=1)), ty[p, 0], ty[p, 1])
            for part in range(2):
                lines[a, part, :, p * HALF : (p + 1) * HALF] = result[
                    :, part * HALF : (part + 1) * HALF
                ]
    for a in range(3):
        for q in range(2):
            values = []
            for part in range(2):
                top, bottom = lines[a, part, :HALF], lines[a, part, HALF:]
                values.append(top - bottom if q else top + bottom)
            result = three_pass(txt[q, 0], txt[q, 1], *split(jnp.concatenate(values, axis=0)))
            for part in range(2):
                modes[a, part, q * HALF : (q + 1) * HALF] = result[
                    part * HALF : (part + 1) * HALF
                ]

    m = pl.program_id(0)
    bin_third = where[1] + m
    kthird = bin_third.astype(jnp.float32)
    scale = jnp.where(bin_third == 0, factor, 2.0 * factor)
    scale = jnp.where(m < live, scale, 0.0)
    chunk = 32
    lane = lax.broadcasted_iota(jnp.int32, (1, HALF), 1)
    seconds = []
    for odd in odds:
        bin_second = 2 * lane + odd
        ksecond = jnp.where(bin_second < HALF, bin_second, bin_second - G).astype(jnp.float32)
        seconds.append((ksecond, jnp.where(bin_second == HALF, 0.0, scale)))

    def project(i, carry):
        rows = pl.ds(pl.multiple_of(i * chunk, chunk), chunk)
        at = lax.broadcasted_iota(jnp.int32, (chunk, 1), 0) + i * chunk
        bin_first = jnp.where(at < HALF, 2 * at, 2 * at - (G - 1))
        kfirst = jnp.where(bin_first < HALF, bin_first, bin_first - G).astype(jnp.float32)
        kept = jnp.where(bin_first == HALF, 0.0, 1.0)
        kfirst, kept = (jnp.broadcast_to(k, (chunk, HALF)) for k in (kfirst, kept))
        partly = kfirst * kfirst + kthird * kthird
        for p, (ksecond, weight) in enumerate(seconds):
            at = slice(p * HALF, (p + 1) * HALF)
            squared = partly + ksecond * ksecond
            shifted = squared + screen_shift
            floored = jnp.maximum(squared, 1.0)
            both = 1.0 / (shifted * floored)
            inverse = shifted * both
            weighting = floored * both * (kept * weight)
            for part in range(2):
                u, v, w = (modes[a, part, rows, at] for a in range(3))
                inner = (kfirst * u + ksecond * v + kthird * w) * inverse
                lines[0, part, rows, at] = (u - kfirst * inner) * weighting
                lines[1, part, rows, at] = (v - ksecond * inner) * weighting
                lines[2, part, rows, at] = (w - kthird * inner) * weighting
        return carry

    lax.fori_loop(0, G // chunk, project, 0)

    for a in range(3):
        results = []
        for q in range(2):
            values = [lines[a, part, q * HALF : (q + 1) * HALF] for part in range(2)]
            results.append(
                three_pass(tx[q, 0], tx[q, 1], *split(jnp.concatenate(values, axis=0)))
            )
        for part in range(2):
            even, odd = (r[part * HALF : (part + 1) * HALF] for r in results)
            modes[a, part, :HALF] = even + odd
            modes[a, part, HALF:] = even - odd
    for a in range(3):
        near = far = None
        for p in range(pars):
            values = [modes[a, part, :, p * HALF : (p + 1) * HALF] for part in range(2)]
            result = three_pass(*split(jnp.concatenate(values, axis=1)), tyt[p, 0], tyt[p, 1])
            near = result if near is None else near + result
            far = signs[p] * result if far is None else far + signs[p] * result
        for part in range(2):
            out[0, a, 0, part] = near[:, part * HALF : (part + 1) * HALF]
            out[1, a, 0, part] = far[:, part * HALF : (part + 1) * HALF]


def gather_kernel(wide, high, where, *refs):
    *sources, phases, field, mine, other, stencils, lines, found, results = refs
    _, parts, slab, _ = field.shape
    cols, _, clusters = stencils.shape
    ordered(wide, high, where, sources, stencils)
    bins = parts // 3
    span = G // cols
    corner = (pl.program_id(0) * slab).astype(jnp.float32)
    for side in range(2):
        for v in range(parts):
            lines[side, pl.ds(v, slab, stride=parts), :] = field[side, v]
    halves = [split(lines[side]) for side in range(2)]
    rows = lax.broadcasted_iota(jnp.int32, (2 * span, clusters), 0)
    rows = jnp.where(rows < span, rows, rows - span).astype(jnp.float32)
    for c in range(cols):
        first = stencils[c, SAMPLES : SAMPLES + 1, :] - corner
        second = stencils[c, SAMPLES + 1 : SAMPLES + 2, :] - c * span
        hot = jnp.concatenate(
            [jnp.where(rows == second + y, 1.0, 0.0) for y in range(SIDE)], axis=1
        ).astype(jnp.bfloat16)
        side, start = divmod(c * span, HALF)
        pair = [half[:, start : start + span] for half in halves[side]]
        found[c % 2] = dot(jnp.concatenate(pair, axis=1), hot)
        target = (c + where[0]) % 2, (c // 2) ^ where[4]
        tall = jnp.broadcast_to(first, (8, clusters))
        for y in range(SIDE):
            lanes = slice(y * clusters, (y + 1) * clusters)
            sums = [[jnp.zeros((8, clusters), jnp.float32)] * (parts // 8) for _ in range(SIDE)]
            chosen = {}
            for cell in range(slab):
                if cell <= slab - SIDE:
                    chosen[cell] = tall == cell
                for j in range(parts // 8):
                    at = cell * parts + j * 8
                    value = found[c % 2, at : at + 8, lanes]
                    for x in range(SIDE):
                        if cell - x in chosen:
                            sums[x][j] = jnp.where(chosen[cell - x], value, sums[x][j])
            for x in range(SIDE):
                total = jnp.concatenate(sums[x], axis=0)
                for a in range(3):
                    mode = total[a * bins : (a + 1) * bins]
                    for z in range(SIDE):
                        at = a * STENCIL + x * 9 + y * 3 + z
                        results[*target, at : at + 1, :] = jnp.sum(
                            mode * phases[c, z], axis=0, keepdims=True
                        )
        results[*target, SAMPLES:, :] = jnp.zeros((HEIGHT - SAMPLES, clusters), jnp.float32)
    for j in range(high):
        mine[0, j, 0] = results[0, j]
        other[0, j, 0] = results[1, j]


def per_device(
    density,
    interp_weight,
    proj_weight,
    stencil_corner,
    near_tiles,
    pair_target,
    pair_landing,
    pair_count,
):
    clusters = stencil_corner.shape[1]
    panels = density.shape[1] // clusters
    deep, wide, high = (lax.axis_size(axis) for axis in AXES[:3])
    here = [lax.axis_index(axis) for axis in AXES]
    rows_total = deep * wide
    cols_total = high * lax.axis_size("core")
    devices = rows_total * cols_total
    device = lax.axis_index(AXES)
    slab = G // rows_total
    kept_bins = G // 2
    third_parts = min(devices, kept_bins)
    second_parts = devices // third_parts
    pars = 2 // second_parts
    third_live = kept_bins // third_parts
    bins = max(4, third_live)
    parts = 3 * 2 * bins
    width = pars * HALF
    f32, bf16 = jnp.float32, jnp.bfloat16

    charges = density.reshape(3, clusters, panels)
    packed = pl.pallas_call(
        spread_kernel,
        out_shape=jax.ShapeDtypeStruct((HEIGHT, clusters), f32),
        name="spread",
    )(density, interp_weight, stencil_corner)
    line = jnp.stack([packed] + [swapped(packed, "z", o) for o in range(1, deep)])
    sources = [line] + [swapped(line, PLANE, o) for o in range(1, wide * high)]
    sources += [swapped(source, "core", 1) for source in sources]

    factor = 1.0 / math.sqrt(density.shape[1] * devices)
    first_parity = device % second_parts
    where = jnp.stack(
        [here[3], device // second_parts * third_live, here[0], here[1], here[2], first_parity]
    ).astype(jnp.int32)

    tables = half_tables()
    tx = jnp.asarray(tables)
    txt = jnp.asarray(np.ascontiguousarray(np.swapaxes(tables, 2, 3)))
    if pars == 2:
        ty, tyt = tx, txt
    else:
        ty = lax.dynamic_slice_in_dim(tx, first_parity, 1, axis=0)
        tyt = lax.dynamic_slice_in_dim(txt, first_parity, 1, axis=0)

    smem = pl.BlockSpec(memory_space=pltpu.SMEM)
    line_block = pl.BlockSpec((deep, HEIGHT, clusters), lambda r, where: (0, 0, 0))
    phase_row = pl.BlockSpec(
        (cols_total, SIDE, 2 * bins, clusters), lambda r, where: (r, 0, 0, 0)
    )
    slab_block = pl.BlockSpec((2, parts, slab, HALF), lambda r, where: (0, 0, r, 0))
    span = G // cols_total
    field, phases = pl.pallas_call(
        functools.partial(scatter_kernel, third_live, wide, high),
        grid_spec=pltpu.PrefetchScalarGridSpec(
            num_scalar_prefetch=1,
            grid=(rows_total,),
            in_specs=[line_block] * len(sources),
            out_specs=[slab_block, phase_row],
            scratch_shapes=[
                pltpu.VMEM((cols_total, HEIGHT, clusters), f32),
                pltpu.VMEM((cols_total, FINE * span // HALF, slab // FINE * 2 * parts, HALF), f32),
            ],
        ),
        out_shape=[
            jax.ShapeDtypeStruct((2, parts, G, HALF), f32),
            jax.ShapeDtypeStruct((devices, SIDE, 2 * bins, clusters), f32),
        ],
        name="scatter",
    )(where, *sources)

    plane = pl.BlockSpec((2, 3, 1, 2, G, HALF), lambda m: (0, 0, m, 0, 0, 0))
    table = pl.BlockSpec((2, 2, G, G), lambda m: (0, 0, 0, 0))
    table_y = pl.BlockSpec((pars, 2, G, G), lambda m: (0, 0, 0, 0))
    field = pl.pallas_call(
        functools.partial(dft_kernel, factor, third_live),
        grid=(bins,),
        in_specs=[smem, plane, table, table, table_y, table_y],
        out_specs=plane,
        out_shape=jax.ShapeDtypeStruct((2, 3, bins, 2, G, HALF), f32),
        scratch_shapes=[
            pltpu.VMEM((3, 2, G, width), f32),
            pltpu.VMEM((3, 2, G, width), f32),
        ],
        name="spectral",
    )(where, field.reshape(2, 3, bins, 2, G, HALF), tx, txt, ty, tyt)

    sample_block = pl.BlockSpec(
        (1, high, 1, HEIGHT, clusters),
        lambda r, where: ((r % wide) ^ where[3], 0, (r // wide) ^ where[2], 0, 0),
    )
    mine, other = pl.pallas_call(
        functools.partial(gather_kernel, wide, high),
        grid_spec=pltpu.PrefetchScalarGridSpec(
            num_scalar_prefetch=1,
            grid=(rows_total,),
            in_specs=[line_block] * len(sources) + [phase_row, slab_block],
            out_specs=[sample_block] * 2,
            scratch_shapes=[
                pltpu.VMEM((cols_total, HEIGHT, clusters), f32),
                pltpu.VMEM((2, slab * parts, HALF), f32),
                pltpu.VMEM((2, slab * parts, SIDE * clusters), f32),
                pltpu.VMEM((2, high, HEIGHT, clusters), f32),
            ],
        ),
        out_shape=[jax.ShapeDtypeStruct((wide, high, deep, HEIGHT, clusters), f32)] * 2,
        name="gather",
    )(where, *sources, phases, field.reshape(2, parts, G, HALF))
    sampled = (mine + swapped(other, "core", 1)).reshape(wide * high, deep, HEIGHT, clusters)
    line = sampled[0] + sum(swapped(sampled[o], PLANE, o) for o in range(1, wide * high))
    samples = [line[0]] + [swapped(line[o], "z", o) for o in range(1, deep)]
    near = near_field(
        density.reshape(3, clusters, panels), near_tiles, pair_target, pair_count
    )
    vmem = pl.BlockSpec(memory_space=pltpu.VMEM)
    return pl.pallas_call(
        final_kernel,
        in_specs=[smem] + [vmem] * (2 + deep),
        out_shape=jax.ShapeDtypeStruct(density.shape, f32),
        name="final",
    )(pair_landing, near, proj_weight, *samples)


def solution(mesh):
    in_specs = (
        P(None, AXES),
        P(None, AXES),
        P(None, AXES),
        P(None, AXES),
        P(AXES, None, None, None, None),
        P(AXES),
        P(AXES),
        P(AXES),
    )
    rows_total, cols_total = (mesh.shape[axis] for axis in ("row", "col"))
    high = cols_total // 2
    wide = high if rows_total % high == 0 else 1
    split_mesh = jax.sharding.Mesh(
        mesh.devices.reshape(rows_total // wide, wide, high, 2), AXES
    )
    return jax.shard_map(
        per_device, mesh=split_mesh, in_specs=in_specs, out_specs=P(None, AXES), check_vma=False
    )
```

```python
import functools
import math

import jax
import jax.numpy as jnp
import numpy as np
from jax import lax
from jax.experimental import pallas as pl
from jax.experimental.pallas import tpu as pltpu
from jax.sharding import PartitionSpec as P

G = 256
HALF = G // 2
STENCIL = 27
SIDE = 3
FINE = 4
SAMPLES = 3 * STENCIL
HEIGHT = 88
TILE = 16
ROW = ("z", "x")
PLANE = ("x", "y")
AXES = ("z", "x", "y", "core")

screen_shift = 0.5


def swapped(values, axes, offset):
    count = lax.axis_size(axes)
    return lax.ppermute(values, axes, [(i, i ^ offset) for i in range(count)])


def in_vmem(values):
    return pltpu.with_memory_space_constraint(values, pltpu.VMEM)


def row_shift(values, by):
    count = lax.axis_size(ROW)
    return lax.ppermute(values, ROW, [(i, (i + by) % count) for i in range(count)])


def near_field(charges, near_tiles, pair_target, pair_count):
    panels = charges.shape[2]
    rounded = charges.astype(jnp.bfloat16)
    slot_total = pair_target.shape[0]
    slot_group = slot_total // 3
    picked = rounded[:, pair_target, :]
    partial_value = jnp.einsum(
        "qabij,aqi->qbj", near_tiles, picked, preferred_element_type=jnp.float32
    )
    live_mask = jnp.arange(slot_total, dtype=jnp.int32) < pair_count[0]
    partial_value = jnp.where(
        live_mask[:, None, None], partial_value, jnp.zeros_like(partial_value)
    )
    leaving = partial_value[slot_group:].reshape(slot_group, 2, 3, panels)
    crossing = jnp.stack([row_shift(leaving[:, 0], -1), row_shift(leaving[:, 1], 1)], axis=1)
    return jnp.concatenate(
        [partial_value[:slot_group], crossing.reshape(2 * slot_group, 3, panels)], axis=0
    )


def half_tables():
    cells = np.arange(HALF)
    parts = []
    for parity in range(2):
        product = cells[:, None] * (2 * cells[None, :] + parity) % G
        angles = product * (2.0 * np.pi / G)
        cosines, sines = np.cos(angles), np.sin(angles)
        table = np.block([[cosines, -sines], [sines, cosines]]).astype(np.float32)
        high = table.astype(jnp.bfloat16)
        low = (table - high.astype(np.float32)).astype(jnp.bfloat16)
        parts.append(np.stack([high, low]))
    return np.stack(parts)


def split(values):
    high = values.astype(jnp.bfloat16)
    low = (values - high.astype(jnp.float32)).astype(jnp.bfloat16)
    return high, low


def dot(left, right):
    return jnp.dot(left, right, preferred_element_type=jnp.float32)


def three_pass(left_high, left_low, right_high, right_low):
    return (
        dot(left_high, right_low) + dot(left_low, right_high) + dot(left_high, right_high)
    )


def spread_kernel(density, weights, corners, out):
    clusters = corners.shape[1]
    panels = density.shape[1] // clusters
    unroll = 8
    lane = lax.broadcasted_iota(jnp.int32, (STENCIL, clusters), 1)

    def some(i, sums):
        for j in range(unroll):
            k = i * unroll + j
            at = pl.ds(pl.multiple_of(k * panels, panels), panels)
            weight = weights[:, at]
            sums = tuple(
                jnp.where(
                    lane == k,
                    jnp.sum(weight * density[a : a + 1, at], axis=1, keepdims=True),
                    sums[a],
                )
                for a in range(3)
            )
        return sums

    blank = jnp.zeros((STENCIL, clusters), jnp.float32)
    sums = lax.fori_loop(0, clusters // unroll, some, (blank, blank, blank))
    for a in range(3):
        out[a * STENCIL : (a + 1) * STENCIL, :] = sums[a]
    out[SAMPLES : SAMPLES + 3, :] = corners[...].astype(jnp.float32)
    out[SAMPLES + 3 :, :] = jnp.zeros((HEIGHT - SAMPLES - 3, clusters), jnp.float32)


def final_kernel(landing, near, weights, *refs):
    *samples, out = refs
    clusters = samples[0].shape[1]
    panels = weights.shape[1] // clusters
    total = sum(sample[...] for sample in samples[1:]) + samples[0][...]
    columns = [total[a * STENCIL : (a + 1) * STENCIL] for a in range(3)]
    for k in range(clusters):
        at = slice(k * panels, (k + 1) * panels)
        weight = weights[:, at]
        for a in range(3):
            out[a : a + 1, at] = jnp.sum(
                columns[a][:, k : k + 1] * weight, axis=0, keepdims=True
            )
    for q in range(near.shape[0]):
        at = pl.ds(pl.multiple_of(landing[q] * panels, panels), panels)
        out[:, at] = out[:, at] + near[q]


def ordered(wide, high, where, sources, stencils):
    row = pl.program_id(0)
    deep = (row // wide) ^ where[2]
    for o in range(wide * high):

        @pl.when((row % wide) ^ where[3] == o // high)
        def _():
            y = (o % high) ^ where[4]
            stencils[2 * y + where[0]] = sources[o][deep]
            stencils[2 * y + 1 - where[0]] = sources[wide * high + o][deep]


def cosine(turns):
    turns = turns & (G - 1)
    turns = jnp.minimum(turns, G - turns)
    flipped = turns > G // 4
    angle = jnp.where(flipped, G // 2 - turns, turns).astype(jnp.float32) * (2.0 * math.pi / G)
    square = angle * angle
    total = jnp.full_like(square, 1.0 / math.factorial(12))
    for order in (10, 8, 6, 4, 2, 0):
        total = total * square + (-1.0) ** (order // 2) / math.factorial(order)
    return jnp.where(flipped, -total, total)


def regrouped(values, span, left):
    if len(values) == 2:
        turned = [pltpu.roll(value, span, axis=1) for value in values]
        return [
            jnp.where(left, values[0], turned[1]),
            jnp.where(left, turned[0], values[1]),
        ]
    return [
        jnp.concatenate([value[:, i * span : (i + 1) * span] for value in values], axis=1)
        for i in range(len(values))
    ]


def scatter_kernel(live, wide, high, where, *refs):
    *sources, out, phases, stencils, total = refs
    sides, parts, _, lanes = out.shape
    cols, _, clusters = stencils.shape
    span = G // cols
    slab = total.shape[2] // (2 * parts) * FINE
    coarse_cells = slab // FINE
    corner = pl.program_id(0) * slab
    ordered(wide, high, where, sources, stencils)
    bins = lax.broadcasted_iota(jnp.int32, phases.shape[2:], 0)
    waves = bins // 2 + where[1]
    quarter = bins % 2 * (G // 4)
    kept = bins < 2 * live
    bf16 = jnp.bfloat16
    column = lax.broadcasted_iota(jnp.int32, (TILE, clusters), 0)
    ones = jnp.ones((TILE, clusters), bf16)
    zeros = jnp.zeros((TILE, clusters), bf16)
    for c in range(cols):
        first, second, third = (
            stencils[c, SAMPLES + i : SAMPLES + i + 1, :].astype(jnp.int32) for i in range(3)
        )
        for z in range(SIDE):
            phases[c, z] = jnp.where(kept, cosine((third + z) * waves + quarter), 0.0)
        phases[c, SIDE, :2] = stencils[c, SAMPLES : SAMPLES + 2, :]
        hots, spreads = [], []
        for x in range(SIDE):
            cell = first - corner + x
            fine = (cell & (FINE - 1)) * span + second - c * span
            fine = jnp.broadcast_to(fine, (TILE, clusters))
            coarse = jnp.broadcast_to(cell // FINE, (TILE, clusters)).astype(jnp.int16)
            for y in range(SIDE):
                target = (fine + y).astype(jnp.int16)
                hots.append(
                    jnp.concatenate(
                        [
                            jnp.where((column + j).astype(jnp.int16) == target, ones, zeros)
                            for j in range(0, FINE * span, TILE)
                        ],
                        axis=0,
                    )
                )
                modes = []
                for a in range(3):
                    row = a * STENCIL + x * 9 + y * 3
                    modes.append(
                        sum(
                            stencils[c, row + z : row + z + 1, :] * phases[c, z]
                            for z in range(SIDE)
                        )
                    )
                modes = jnp.concatenate(modes, axis=0)
                low = modes - modes.astype(bf16).astype(jnp.float32)
                tile = jnp.concatenate([modes, low], axis=0).astype(bf16)
                pieces = []
                for h in range(coarse_cells):
                    chosen = coarse == jnp.asarray(h, jnp.int16)
                    for j in range(0, 2 * parts, TILE):
                        pieces.append(jnp.where(chosen, tile[j : j + TILE], zeros))
                spreads.append(jnp.concatenate(pieces, axis=0))
        result = lax.dot_general(
            jnp.concatenate(spreads, axis=1),
            jnp.concatenate(hots, axis=1),
            (((1,), (1,)), ((), ())),
            preferred_element_type=jnp.float32,
        )
        for part in range(total.shape[1]):
            total[c, part] = result[:, part * lanes : (part + 1) * lanes]
    across = lanes // span
    left = lax.broadcasted_iota(jnp.int32, (coarse_cells, lanes), 1) < span
    for part in range(total.shape[1]):
        for v in range(parts):
            for side in range(sides):
                values = [
                    total[c, part, pl.ds(v, coarse_cells, stride=2 * parts), :]
                    + total[c, part, pl.ds(parts + v, coarse_cells, stride=2 * parts), :]
                    for c in range(side * across, (side + 1) * across)
                ]
                for i, row in enumerate(regrouped(values, span, left)):
                    at = pl.ds(corner + part * across + i, coarse_cells, stride=FINE)
                    out[side, v, at, :] = row


def dft_kernel(factor, live, pars, where, field, *refs):
    *tables, out, lines, modes = refs
    tx, txt = tables[:2]
    ty, tyt = tables[-2:]
    m = pl.program_id(0)
    width = pars * HALF
    odds = [where[5] + p for p in range(pars)]
    signs = [1.0 - 2.0 * odd.astype(jnp.float32) for odd in odds]

    for p in range(pars):
        for a in range(3):
            values = [field[0, a, m, i] + signs[p] * field[1, a, m, i] for i in range(2)]
            result = three_pass(*split(jnp.concatenate(values, axis=1)), ty[p, 0], ty[p, 1])
            for part in range(2):
                lines[a, part, :, p * HALF : (p + 1) * HALF] = result[
                    :, part * HALF : (part + 1) * HALF
                ]
    for a in range(3):
        for q in range(2):
            values = []
            for part in range(2):
                top, bottom = lines[a, part, :HALF], lines[a, part, HALF:]
                values.append(top - bottom if q else top + bottom)
            result = three_pass(txt[q, 0], txt[q, 1], *split(jnp.concatenate(values, axis=0)))
            for part in range(2):
                modes[a, part, q * HALF : (q + 1) * HALF] = result[
                    part * HALF : (part + 1) * HALF
                ]

    bin_third = where[1] + m
    kthird = bin_third.astype(jnp.float32)
    scale = jnp.where(bin_third == 0, factor, 2.0 * factor)
    scale = jnp.where(m < live, scale, 0.0)
    chunk = 32
    lane = lax.broadcasted_iota(jnp.int32, (1, HALF), 1)
    seconds = []
    for odd in odds:
        bin_second = 2 * lane + odd
        ksecond = jnp.where(bin_second < HALF, bin_second, bin_second - G).astype(jnp.float32)
        seconds.append((ksecond, jnp.where(bin_second == HALF, 0.0, scale)))

    def project(i, carry):
        rows = pl.ds(pl.multiple_of(i * chunk, chunk), chunk)
        at = lax.broadcasted_iota(jnp.int32, (chunk, 1), 0) + i * chunk
        bin_first = jnp.where(at < HALF, 2 * at, 2 * at - (G - 1))
        kfirst = jnp.where(bin_first < HALF, bin_first, bin_first - G).astype(jnp.float32)
        kept = jnp.where(bin_first == HALF, 0.0, 1.0)
        kfirst, kept = (jnp.broadcast_to(k, (chunk, HALF)) for k in (kfirst, kept))
        partly = kfirst * kfirst + kthird * kthird
        for p, (ksecond, weight) in enumerate(seconds):
            at = slice(p * HALF, (p + 1) * HALF)
            squared = partly + ksecond * ksecond
            shifted = squared + screen_shift
            floored = jnp.maximum(squared, 1.0)
            both = 1.0 / (shifted * floored)
            inverse = shifted * both
            weighting = floored * both * (kept * weight)
            for part in range(2):
                u, v, w = (modes[a, part, rows, at] for a in range(3))
                inner = (kfirst * u + ksecond * v + kthird * w) * inverse
                lines[0, part, rows, at] = (u - kfirst * inner) * weighting
                lines[1, part, rows, at] = (v - ksecond * inner) * weighting
                lines[2, part, rows, at] = (w - kthird * inner) * weighting
        return carry

    lax.fori_loop(0, G // chunk, project, 0)

    for a in range(3):
        results = []
        for q in range(2):
            values = [lines[a, part, q * HALF : (q + 1) * HALF] for part in range(2)]
            results.append(
                three_pass(tx[q, 0], tx[q, 1], *split(jnp.concatenate(values, axis=0)))
            )
        for part in range(2):
            even, odd = (r[part * HALF : (part + 1) * HALF] for r in results)
            modes[a, part, :HALF] = even + odd
            modes[a, part, HALF:] = even - odd
    for a in range(3):
        near = far = None
        for p in range(pars):
            values = [modes[a, part, :, p * HALF : (p + 1) * HALF] for part in range(2)]
            result = three_pass(*split(jnp.concatenate(values, axis=1)), tyt[p, 0], tyt[p, 1])
            near = result if near is None else near + result
            far = signs[p] * result if far is None else far + signs[p] * result
        for part in range(2):
            out[0, a, m, part] = near[:, part * HALF : (part + 1) * HALF]
            out[1, a, m, part] = far[:, part * HALF : (part + 1) * HALF]


def gather_kernel(where, phases, field, mine, other, lines, found, results):
    parts = field.shape[1]
    cols, _, _, clusters = phases.shape
    high = mine.shape[1]
    slab = lines.shape[1] // parts
    start_row = pl.multiple_of(pl.program_id(0) * slab, slab)
    bins = parts // 3
    span = G // cols
    corner = (pl.program_id(0) * slab).astype(jnp.float32)
    for side in range(2):
        for v in range(parts):
            lines[side, pl.ds(v, slab, stride=parts), :] = field[side, v, pl.ds(start_row, slab), :]
    halves = [split(lines[side]) for side in range(2)]
    rows = lax.broadcasted_iota(jnp.int32, (2 * span, clusters), 0)
    rows = jnp.where(rows < span, rows, rows - span).astype(jnp.float32)
    for c in range(cols):
        first = phases[c, SIDE, :1] - corner
        second = phases[c, SIDE, 1:2] - c * span
        hot = jnp.concatenate(
            [jnp.where(rows == second + y, 1.0, 0.0) for y in range(SIDE)], axis=1
        ).astype(jnp.bfloat16)
        side, start = divmod(c * span, HALF)
        pair = [half[:, start : start + span] for half in halves[side]]
        found[c % 2] = dot(jnp.concatenate(pair, axis=1), hot)
        target = (c + where[0]) % 2, (c // 2) ^ where[4]
        tall = jnp.broadcast_to(first, (8, clusters))
        for y in range(SIDE):
            lanes = slice(y * clusters, (y + 1) * clusters)
            sums = [[jnp.zeros((8, clusters), jnp.float32)] * (parts // 8) for _ in range(SIDE)]
            chosen = {}
            for cell in range(slab):
                if cell <= slab - SIDE:
                    chosen[cell] = tall == cell
                for j in range(parts // 8):
                    at = cell * parts + j * 8
                    value = found[c % 2, at : at + 8, lanes]
                    for x in range(SIDE):
                        if cell - x in chosen:
                            sums[x][j] = jnp.where(chosen[cell - x], value, sums[x][j])
            for x in range(SIDE):
                total = jnp.concatenate(sums[x], axis=0)
                for a in range(3):
                    mode = total[a * bins : (a + 1) * bins]
                    for z in range(SIDE):
                        at = a * STENCIL + x * 9 + y * 3 + z
                        results[*target, at : at + 1, :] = jnp.sum(
                            mode * phases[c, z], axis=0, keepdims=True
                        )
        results[*target, SAMPLES:, :] = jnp.zeros((HEIGHT - SAMPLES, clusters), jnp.float32)
    for j in range(high):
        mine[0, j, 0] = results[0, j]
        other[0, j, 0] = results[1, j]


def per_device(
    density,
    interp_weight,
    proj_weight,
    stencil_corner,
    near_tiles,
    pair_target,
    pair_landing,
    pair_count,
):
    clusters = stencil_corner.shape[1]
    panels = density.shape[1] // clusters
    deep, wide, high = (lax.axis_size(axis) for axis in AXES[:3])
    here = [lax.axis_index(axis) for axis in AXES]
    rows_total = deep * wide
    cols_total = high * lax.axis_size("core")
    devices = rows_total * cols_total
    device = lax.axis_index(AXES)
    slab = G // rows_total
    kept_bins = G // 2
    third_parts = min(devices, kept_bins)
    second_parts = devices // third_parts
    pars = 2 // second_parts
    third_live = kept_bins // third_parts
    bins = max(4, third_live)
    parts = 3 * 2 * bins
    width = pars * HALF
    f32, bf16 = jnp.float32, jnp.bfloat16

    charges = density.reshape(3, clusters, panels)
    packed = pl.pallas_call(
        spread_kernel,
        out_shape=jax.ShapeDtypeStruct((HEIGHT, clusters), f32),
        compiler_params=pltpu.CompilerParams(vmem_limit_bytes=24 << 20),
        name="spread",
    )(density, interp_weight, stencil_corner)
    line = jnp.stack([packed] + [swapped(packed, "z", o) for o in range(1, deep)])
    sources = [line] + [swapped(line, PLANE, o) for o in range(1, wide * high)]
    sources += [swapped(source, "core", 1) for source in sources]
    sources = [in_vmem(source) for source in sources]

    factor = 1.0 / math.sqrt(density.shape[1] * devices)
    first_parity = device % second_parts
    where = jnp.stack(
        [here[3], device // second_parts * third_live, here[0], here[1], here[2], first_parity]
    ).astype(jnp.int32)

    tables = half_tables()
    tx = jnp.asarray(tables)
    txt = jnp.asarray(np.ascontiguousarray(np.swapaxes(tables, 2, 3)))
    tables = [tx, txt]
    if pars == 1:
        tables += [lax.dynamic_slice_in_dim(t, first_parity, 1, axis=0) for t in tables]
    tables = [in_vmem(table) for table in tables]

    smem = pl.BlockSpec(memory_space=pltpu.SMEM)
    line_block = pl.BlockSpec(memory_space=pltpu.VMEM)
    phase_row = pl.BlockSpec(
        (cols_total, SIDE + 1, 2 * bins, clusters), lambda r, where: (r, 0, 0, 0)
    )
    vmem = pl.BlockSpec(memory_space=pltpu.VMEM)
    span = G // cols_total
    field, phases = pl.pallas_call(
        functools.partial(scatter_kernel, third_live, wide, high),
        grid_spec=pltpu.PrefetchScalarGridSpec(
            num_scalar_prefetch=1,
            grid=(rows_total,),
            in_specs=[line_block] * len(sources),
            out_specs=[vmem, phase_row],
            scratch_shapes=[
                pltpu.VMEM((cols_total, HEIGHT, clusters), f32),
                pltpu.VMEM((cols_total, FINE * span // HALF, slab // FINE * 2 * parts, HALF), f32),
            ],
        ),
        out_shape=[
            pltpu.VMEM((2, parts, G, HALF), f32),
            jax.ShapeDtypeStruct((devices, SIDE + 1, 2 * bins, clusters), f32),
        ],
        compiler_params=pltpu.CompilerParams(vmem_limit_bytes=24 << 20),
        name="scatter",
    )(where, *sources)

    field = in_vmem(field.reshape(2, 3, bins, 2, G, HALF))
    field = pl.pallas_call(
        functools.partial(dft_kernel, factor, third_live, pars),
        grid=(bins,),
        in_specs=[smem] + [vmem] * (1 + len(tables)),
        out_specs=vmem,
        out_shape=pltpu.VMEM((2, 3, bins, 2, G, HALF), f32),
        scratch_shapes=[
            pltpu.VMEM((3, 2, G, width), f32),
            pltpu.VMEM((3, 2, G, width), f32),
        ],
        compiler_params=pltpu.CompilerParams(vmem_limit_bytes=24 << 20),
        name="spectral",
    )(where, field, *tables)

    sample_block = pl.BlockSpec(
        (1, high, 1, HEIGHT, clusters),
        lambda r, where: ((r % wide) ^ where[3], 0, (r // wide) ^ where[2], 0, 0),
    )
    mine, other = pl.pallas_call(
        gather_kernel,
        grid_spec=pltpu.PrefetchScalarGridSpec(
            num_scalar_prefetch=1,
            grid=(rows_total,),
            in_specs=[phase_row, vmem],
            out_specs=[sample_block] * 2,
            scratch_shapes=[
                pltpu.VMEM((2, slab * parts, HALF), f32),
                pltpu.VMEM((2, slab * parts, SIDE * clusters), f32),
                pltpu.VMEM((2, high, HEIGHT, clusters), f32),
            ],
        ),
        out_shape=[jax.ShapeDtypeStruct((wide, high, deep, HEIGHT, clusters), f32)] * 2,
        compiler_params=pltpu.CompilerParams(vmem_limit_bytes=24 << 20),
        name="gather",
    )(where, phases, in_vmem(field.reshape(2, parts, G, HALF)))
    sampled = (mine + swapped(other, "core", 1)).reshape(wide * high, deep, HEIGHT, clusters)
    line = sampled[0] + sum(swapped(sampled[o], PLANE, o) for o in range(1, wide * high))
    samples = [line[0]] + [swapped(line[o], "z", o) for o in range(1, deep)]
    samples = [in_vmem(sample) for sample in samples]
    near = near_field(
        density.reshape(3, clusters, panels), near_tiles, pair_target, pair_count
    )
    return pl.pallas_call(
        final_kernel,
        in_specs=[smem] + [vmem] * (2 + deep),
        out_shape=jax.ShapeDtypeStruct(density.shape, f32),
        compiler_params=pltpu.CompilerParams(vmem_limit_bytes=24 << 20),
        name="final",
    )(pair_landing, near, in_vmem(proj_weight), *samples)


def solution(mesh):
    in_specs = (
        P(None, AXES),
        P(None, AXES),
        P(None, AXES),
        P(None, AXES),
        P(AXES, None, None, None, None),
        P(AXES),
        P(AXES),
        P(AXES),
    )
    rows_total, cols_total = (mesh.shape[axis] for axis in ("row", "col"))
    high = cols_total // 2
    wide = high if rows_total % high == 0 else 1
    split_mesh = jax.sharding.Mesh(
        mesh.devices.reshape(rows_total // wide, wide, high, 2), AXES
    )
    return jax.shard_map(
        per_device, mesh=split_mesh, in_specs=in_specs, out_specs=P(None, AXES), check_vma=False
    )
```

```python
import functools
import math

import jax
import jax.numpy as jnp
import numpy as np
from jax import lax
from jax.experimental import pallas as pl
from jax.experimental.pallas import tpu as pltpu
from jax.sharding import PartitionSpec as P

G = 256
HALF = G // 2
STENCIL = 27
SIDE = 3
FINE = 4
SAMPLES = 3 * STENCIL
HEIGHT = 88
TILE = 16
ROW = ("z", "x")
PLANE = ("x", "y")
AXES = ("z", "x", "y", "core")

screen_shift = 0.5


def swapped(values, axes, offset):
    count = lax.axis_size(axes)
    return lax.ppermute(values, axes, [(i, i ^ offset) for i in range(count)])


def in_vmem(values):
    return pltpu.with_memory_space_constraint(values, pltpu.VMEM)


def row_shift(values, by):
    count = lax.axis_size(ROW)
    return lax.ppermute(values, ROW, [(i, (i + by) % count) for i in range(count)])


def near_field(charges, near_tiles, pair_target, pair_count):
    panels = charges.shape[2]
    rounded = charges.astype(jnp.bfloat16)
    slot_total = pair_target.shape[0]
    slot_group = slot_total // 3
    picked = rounded[:, pair_target, :]
    partial_value = jnp.einsum(
        "qabij,aqi->qbj", near_tiles, picked, preferred_element_type=jnp.float32
    )
    live_mask = jnp.arange(slot_total, dtype=jnp.int32) < pair_count[0]
    partial_value = jnp.where(
        live_mask[:, None, None], partial_value, jnp.zeros_like(partial_value)
    )
    leaving = partial_value[slot_group:].reshape(slot_group, 2, 3, panels)
    crossing = jnp.stack([row_shift(leaving[:, 0], -1), row_shift(leaving[:, 1], 1)], axis=1)
    return jnp.concatenate(
        [partial_value[:slot_group], crossing.reshape(2 * slot_group, 3, panels)], axis=0
    )


def half_tables():
    cells = np.arange(HALF)
    parts = []
    for parity in range(2):
        product = cells[:, None] * (2 * cells[None, :] + parity) % G
        angles = product * (2.0 * np.pi / G)
        cosines, sines = np.cos(angles), np.sin(angles)
        table = np.block([[cosines, -sines], [sines, cosines]]).astype(np.float32)
        high = table.astype(jnp.bfloat16)
        low = (table - high.astype(np.float32)).astype(jnp.bfloat16)
        parts.append(np.stack([high, low]))
    return np.stack(parts)


def split(values):
    high = values.astype(jnp.bfloat16)
    low = (values - high.astype(jnp.float32)).astype(jnp.bfloat16)
    return high, low


def dot(left, right):
    return jnp.dot(left, right, preferred_element_type=jnp.float32)


def three_pass(left_high, left_low, right_high, right_low):
    return (
        dot(left_high, right_low) + dot(left_low, right_high) + dot(left_high, right_high)
    )


def spread_kernel(density, weights, corners, out):
    clusters = corners.shape[1]
    panels = density.shape[1] // clusters
    unroll = 8
    lane = lax.broadcasted_iota(jnp.int32, (STENCIL, clusters), 1)

    def some(i, sums):
        for j in range(unroll):
            k = i * unroll + j
            at = pl.ds(pl.multiple_of(k * panels, panels), panels)
            weight = weights[:, at]
            sums = tuple(
                jnp.where(
                    lane == k,
                    jnp.sum(weight * density[a : a + 1, at], axis=1, keepdims=True),
                    sums[a],
                )
                for a in range(3)
            )
        return sums

    blank = jnp.zeros((STENCIL, clusters), jnp.float32)
    sums = lax.fori_loop(0, clusters // unroll, some, (blank, blank, blank))
    for a in range(3):
        out[a * STENCIL : (a + 1) * STENCIL, :] = sums[a]
    out[SAMPLES : SAMPLES + 3, :] = corners[...].astype(jnp.float32)
    out[SAMPLES + 3 :, :] = jnp.zeros((HEIGHT - SAMPLES - 3, clusters), jnp.float32)


def final_kernel(landing, near, weights, *refs):
    *samples, out = refs
    clusters = samples[0].shape[1]
    panels = weights.shape[1] // clusters
    total = sum(sample[...] for sample in samples[1:]) + samples[0][...]
    columns = [total[a * STENCIL : (a + 1) * STENCIL] for a in range(3)]
    for k in range(clusters):
        at = slice(k * panels, (k + 1) * panels)
        weight = weights[:, at]
        for a in range(3):
            out[a : a + 1, at] = jnp.sum(
                columns[a][:, k : k + 1] * weight, axis=0, keepdims=True
            )
    for q in range(near.shape[0]):
        at = pl.ds(pl.multiple_of(landing[q] * panels, panels), panels)
        out[:, at] = out[:, at] + near[q]


def ordered(group, high, step, where, sources, stencils):
    deep = (step // group) ^ where[2]
    for o in range(group * high):

        def fill(o=o):
            y = (o % high) ^ where[4]
            stencils[2 * y + where[0]] = sources[o][deep]
            stencils[2 * y + 1 - where[0]] = sources[group * high + o][deep]

        if group == 1:
            fill()
        else:
            pl.when(step % group == o // high)(fill)


def cosine(turns):
    turns = turns & (G - 1)
    turns = jnp.minimum(turns, G - turns)
    flipped = turns > G // 4
    angle = jnp.where(flipped, G // 2 - turns, turns).astype(jnp.float32) * (2.0 * math.pi / G)
    square = angle * angle
    total = jnp.full_like(square, 1.0 / math.factorial(12))
    for order in (10, 8, 6, 4, 2, 0):
        total = total * square + (-1.0) ** (order // 2) / math.factorial(order)
    return jnp.where(flipped, -total, total)


def regrouped(values, span, left):
    if len(values) == 2:
        turned = [pltpu.roll(value, span, axis=1) for value in values]
        return [
            jnp.where(left, values[0], turned[1]),
            jnp.where(left, turned[0], values[1]),
        ]
    return [
        jnp.concatenate([value[:, i * span : (i + 1) * span] for value in values], axis=1)
        for i in range(len(values))
    ]


def scatter_kernel(live, wide, high, begin, end, where, *refs):
    *sources, out, phases, stencils, total = refs
    step = pl.program_id(0)
    group = end - begin
    row = step // group * wide + ((begin + step % group) ^ where[3])
    sides, parts, _, lanes = out.shape
    cols, _, clusters = stencils.shape
    span = G // cols
    slab = total.shape[2] // (2 * parts) * FINE
    coarse_cells = slab // FINE
    corner = row * slab
    ordered(group, high, step, where, sources[: 2 * group * high], stencils)
    bins = lax.broadcasted_iota(jnp.int32, phases.shape[2:], 0)
    waves = bins // 2 + where[1]
    quarter = bins % 2 * (G // 4)
    kept = bins < 2 * live
    bf16 = jnp.bfloat16
    column = lax.broadcasted_iota(jnp.int32, (TILE, clusters), 0)
    ones = jnp.ones((TILE, clusters), bf16)
    zeros = jnp.zeros((TILE, clusters), bf16)
    for c in range(cols):
        first, second, third = (
            stencils[c, SAMPLES + i : SAMPLES + i + 1, :].astype(jnp.int32) for i in range(3)
        )
        turned = []
        for z in range(SIDE):
            turned.append(jnp.where(kept, cosine((third + z) * waves + quarter), 0.0))
            phases[row * cols + c, z] = turned[z]
        phases[row * cols + c, SIDE, :2] = stencils[c, SAMPLES : SAMPLES + 2, :]
        hots, spreads = [], []
        for x in range(SIDE):
            cell = first - corner + x
            fine = (cell & (FINE - 1)) * span + second - c * span
            fine = jnp.broadcast_to(fine, (TILE, clusters))
            coarse = jnp.broadcast_to(cell // FINE, (TILE, clusters)).astype(jnp.int16)
            for y in range(SIDE):
                target = (fine + y).astype(jnp.int16)
                hots.append(
                    jnp.concatenate(
                        [
                            jnp.where((column + j).astype(jnp.int16) == target, ones, zeros)
                            for j in range(0, FINE * span, TILE)
                        ],
                        axis=0,
                    )
                )
                modes = []
                for a in range(3):
                    at = a * STENCIL + x * 9 + y * 3
                    modes.append(
                        sum(
                            stencils[c, at + z : at + z + 1, :] * turned[z]
                            for z in range(SIDE)
                        )
                    )
                modes = jnp.concatenate(modes, axis=0)
                low = modes - modes.astype(bf16).astype(jnp.float32)
                tile = jnp.concatenate([modes, low], axis=0).astype(bf16)
                pieces = []
                for h in range(coarse_cells):
                    chosen = coarse == jnp.asarray(h, jnp.int16)
                    for j in range(0, 2 * parts, TILE):
                        pieces.append(jnp.where(chosen, tile[j : j + TILE], zeros))
                spreads.append(jnp.concatenate(pieces, axis=0))
        result = lax.dot_general(
            jnp.concatenate(spreads, axis=1),
            jnp.concatenate(hots, axis=1),
            (((1,), (1,)), ((), ())),
            preferred_element_type=jnp.float32,
        )
        for part in range(total.shape[1]):
            total[c, part] = result[:, part * lanes : (part + 1) * lanes]
    across = lanes // span
    left = lax.broadcasted_iota(jnp.int32, (coarse_cells, lanes), 1) < span
    for part in range(total.shape[1]):
        for v in range(parts):
            for side in range(sides):
                values = [
                    total[c, part, pl.ds(v, coarse_cells, stride=2 * parts), :]
                    + total[c, part, pl.ds(parts + v, coarse_cells, stride=2 * parts), :]
                    for c in range(side * across, (side + 1) * across)
                ]
                for i, value in enumerate(regrouped(values, span, left)):
                    at = pl.ds(corner + part * across + i, coarse_cells, stride=FINE)
                    out[side, v, at, :] = value


def dft_kernel(factor, live, pars, where, field, *refs):
    *tables, out, lines, modes = refs
    tx, txt = tables[:2]
    ty, tyt = tables[-2:]
    m = pl.program_id(0)
    width = pars * HALF
    odds = [where[5] + p for p in range(pars)]
    signs = [1.0 - 2.0 * odd.astype(jnp.float32) for odd in odds]

    for p in range(pars):
        for a in range(3):
            values = [field[0, a, m, i] + signs[p] * field[1, a, m, i] for i in range(2)]
            result = three_pass(*split(jnp.concatenate(values, axis=1)), ty[p, 0], ty[p, 1])
            for part in range(2):
                lines[a, part, :, p * HALF : (p + 1) * HALF] = result[
                    :, part * HALF : (part + 1) * HALF
                ]
    for a in range(3):
        for q in range(2):
            values = []
            for part in range(2):
                top, bottom = lines[a, part, :HALF], lines[a, part, HALF:]
                values.append(top - bottom if q else top + bottom)
            result = three_pass(txt[q, 0], txt[q, 1], *split(jnp.concatenate(values, axis=0)))
            for part in range(2):
                modes[a, part, q * HALF : (q + 1) * HALF] = result[
                    part * HALF : (part + 1) * HALF
                ]

    bin_third = where[1] + m
    kthird = bin_third.astype(jnp.float32)
    scale = jnp.where(bin_third == 0, factor, 2.0 * factor)
    scale = jnp.where(m < live, scale, 0.0)
    chunk = 32
    lane = lax.broadcasted_iota(jnp.int32, (1, HALF), 1)
    seconds = []
    for odd in odds:
        bin_second = 2 * lane + odd
        ksecond = jnp.where(bin_second < HALF, bin_second, bin_second - G).astype(jnp.float32)
        seconds.append((ksecond, jnp.where(bin_second == HALF, 0.0, scale)))

    def project(i, carry):
        rows = pl.ds(pl.multiple_of(i * chunk, chunk), chunk)
        at = lax.broadcasted_iota(jnp.int32, (chunk, 1), 0) + i * chunk
        bin_first = jnp.where(at < HALF, 2 * at, 2 * at - (G - 1))
        kfirst = jnp.where(bin_first < HALF, bin_first, bin_first - G).astype(jnp.float32)
        kept = jnp.where(bin_first == HALF, 0.0, 1.0)
        kfirst, kept = (jnp.broadcast_to(k, (chunk, HALF)) for k in (kfirst, kept))
        partly = kfirst * kfirst + kthird * kthird
        for p, (ksecond, weight) in enumerate(seconds):
            at = slice(p * HALF, (p + 1) * HALF)
            squared = partly + ksecond * ksecond
            shifted = squared + screen_shift
            floored = jnp.maximum(squared, 1.0)
            both = 1.0 / (shifted * floored)
            inverse = shifted * both
            weighting = floored * both * (kept * weight)
            for part in range(2):
                u, v, w = (modes[a, part, rows, at] for a in range(3))
                inner = (kfirst * u + ksecond * v + kthird * w) * inverse
                lines[0, part, rows, at] = (u - kfirst * inner) * weighting
                lines[1, part, rows, at] = (v - ksecond * inner) * weighting
                lines[2, part, rows, at] = (w - kthird * inner) * weighting
        return carry

    lax.fori_loop(0, G // chunk, project, 0)

    for a in range(3):
        results = []
        for q in range(2):
            values = [lines[a, part, q * HALF : (q + 1) * HALF] for part in range(2)]
            results.append(
                three_pass(tx[q, 0], tx[q, 1], *split(jnp.concatenate(values, axis=0)))
            )
        for part in range(2):
            even, odd = (r[part * HALF : (part + 1) * HALF] for r in results)
            modes[a, part, :HALF] = even + odd
            modes[a, part, HALF:] = even - odd
    for a in range(3):
        near = far = None
        for p in range(pars):
            values = [modes[a, part, :, p * HALF : (p + 1) * HALF] for part in range(2)]
            result = three_pass(*split(jnp.concatenate(values, axis=1)), tyt[p, 0], tyt[p, 1])
            near = result if near is None else near + result
            far = signs[p] * result if far is None else far + signs[p] * result
        for part in range(2):
            out[0, a, m, part] = near[:, part * HALF : (part + 1) * HALF]
            out[1, a, m, part] = far[:, part * HALF : (part + 1) * HALF]


def gather_kernel(where, phases, field, mine, other, lines, found, results):
    parts = field.shape[1]
    cols, _, _, clusters = phases.shape
    high = mine.shape[1]
    slab = lines.shape[1] // parts
    start_row = pl.multiple_of(pl.program_id(0) * slab, slab)
    bins = parts // 3
    span = G // cols
    corner = (pl.program_id(0) * slab).astype(jnp.float32)
    for side in range(2):
        for v in range(parts):
            lines[side, pl.ds(v, slab, stride=parts), :] = field[side, v, pl.ds(start_row, slab), :]
    halves = [split(lines[side]) for side in range(2)]
    rows = lax.broadcasted_iota(jnp.int32, (2 * span, clusters), 0)
    rows = jnp.where(rows < span, rows, rows - span).astype(jnp.float32)
    for c in range(cols):
        first = phases[c, SIDE, :1] - corner
        second = phases[c, SIDE, 1:2] - c * span
        hot = jnp.concatenate(
            [jnp.where(rows == second + y, 1.0, 0.0) for y in range(SIDE)], axis=1
        ).astype(jnp.bfloat16)
        side, start = divmod(c * span, HALF)
        pair = [half[:, start : start + span] for half in halves[side]]
        found[c % 2] = dot(jnp.concatenate(pair, axis=1), hot)
        target = (c + where[0]) % 2, (c // 2) ^ where[4]
        tall = jnp.broadcast_to(first, (8, clusters))
        for y in range(SIDE):
            lanes = slice(y * clusters, (y + 1) * clusters)
            sums = [[jnp.zeros((8, clusters), jnp.float32)] * (parts // 8) for _ in range(SIDE)]
            chosen = {}
            for cell in range(slab):
                if cell <= slab - SIDE:
                    chosen[cell] = tall == cell
                for j in range(parts // 8):
                    at = cell * parts + j * 8
                    value = found[c % 2, at : at + 8, lanes]
                    for x in range(SIDE):
                        if cell - x in chosen:
                            sums[x][j] = jnp.where(chosen[cell - x], value, sums[x][j])
            for x in range(SIDE):
                total = jnp.concatenate(sums[x], axis=0)
                for a in range(3):
                    mode = total[a * bins : (a + 1) * bins]
                    for z in range(SIDE):
                        at = a * STENCIL + x * 9 + y * 3 + z
                        results[*target, at : at + 1, :] = jnp.sum(
                            mode * phases[c, z], axis=0, keepdims=True
                        )
        results[*target, SAMPLES:, :] = jnp.zeros((HEIGHT - SAMPLES, clusters), jnp.float32)
    for j in range(high):
        mine[0, j, 0] = results[0, j]
        other[0, j, 0] = results[1, j]


def per_device(
    density,
    interp_weight,
    proj_weight,
    stencil_corner,
    near_tiles,
    pair_target,
    pair_landing,
    pair_count,
):
    clusters = stencil_corner.shape[1]
    panels = density.shape[1] // clusters
    deep, wide, high = (lax.axis_size(axis) for axis in AXES[:3])
    here = [lax.axis_index(axis) for axis in AXES]
    rows_total = deep * wide
    cols_total = high * lax.axis_size("core")
    devices = rows_total * cols_total
    device = lax.axis_index(AXES)
    slab = G // rows_total
    kept_bins = G // 2
    third_parts = min(devices, kept_bins)
    second_parts = devices // third_parts
    pars = 2 // second_parts
    third_live = kept_bins // third_parts
    bins = max(4, third_live)
    parts = 3 * 2 * bins
    width = pars * HALF
    f32, bf16 = jnp.float32, jnp.bfloat16

    charges = density.reshape(3, clusters, panels)
    packed = pl.pallas_call(
        spread_kernel,
        out_shape=jax.ShapeDtypeStruct((HEIGHT, clusters), f32),
        name="spread",
    )(density, interp_weight, stencil_corner)
    line = jnp.stack([packed] + [swapped(packed, "z", o) for o in range(1, deep)])
    first_parity = device % second_parts
    tables = half_tables()
    tx = jnp.asarray(tables)
    txt = jnp.asarray(np.ascontiguousarray(np.swapaxes(tables, 2, 3)))
    tables = [tx, txt]
    if pars == 1:
        tables += [lax.dynamic_slice_in_dim(t, first_parity, 1, axis=0) for t in tables]
    tables = [in_vmem(table) for table in tables]
    line, *tables = lax.optimization_barrier((line, *tables))
    sources = [line] + [swapped(line, PLANE, o) for o in range(1, wide * high)]

    factor = 1.0 / math.sqrt(density.shape[1] * devices)
    where = jnp.stack(
        [here[3], device // second_parts * third_live, here[0], here[1], here[2], first_parity]
    ).astype(jnp.int32)

    smem = pl.BlockSpec(memory_space=pltpu.SMEM)
    phase_row = pl.BlockSpec(
        (cols_total, SIDE + 1, 2 * bins, clusters), lambda r, where: (r, 0, 0, 0)
    )
    vmem = pl.BlockSpec(memory_space=pltpu.VMEM)
    span = G // cols_total
    filled = ()
    for begin, end in ((0, 1), (1, wide)):
        if begin == end:
            continue
        lines = sources[begin * high : end * high]
        filled, lines = lax.optimization_barrier((filled, lines))
        lines += [swapped(values, "core", 1) for values in lines]
        operands = [in_vmem(values) for values in (*lines, *filled)]
        first_filled = 1 + len(lines)
        filled = pl.pallas_call(
            functools.partial(scatter_kernel, third_live, wide, high, begin, end),
            grid=(deep * (end - begin),),
            in_specs=[smem] + [vmem] * len(operands),
            out_specs=[vmem] * 2,
            out_shape=[
                pltpu.VMEM((2, parts, G, HALF), f32),
                pltpu.VMEM((devices, SIDE + 1, 2 * bins, clusters), f32),
            ],
            scratch_shapes=[
                pltpu.VMEM((cols_total, HEIGHT, clusters), f32),
                pltpu.VMEM((cols_total, FINE * span // HALF, slab // FINE * 2 * parts, HALF), f32),
            ],
            input_output_aliases={first_filled + i: i for i in range(len(filled))},
            compiler_params=pltpu.CompilerParams(vmem_limit_bytes=24 << 20),
            name="scatter",
        )(where, *operands)
    field, phases = filled

    field = in_vmem(field.reshape(2, 3, bins, 2, G, HALF))
    field = pl.pallas_call(
        functools.partial(dft_kernel, factor, third_live, pars),
        grid=(bins,),
        in_specs=[smem] + [vmem] * (1 + len(tables)),
        out_specs=vmem,
        out_shape=pltpu.VMEM((2, 3, bins, 2, G, HALF), f32),
        scratch_shapes=[
            pltpu.VMEM((3, 2, G, width), f32),
            pltpu.VMEM((3, 2, G, width), f32),
        ],
        compiler_params=pltpu.CompilerParams(vmem_limit_bytes=24 << 20),
        name="spectral",
    )(where, field, *tables)

    sample_block = pl.BlockSpec(
        (1, high, 1, HEIGHT, clusters),
        lambda r, where: ((r % wide) ^ where[3], 0, (r // wide) ^ where[2], 0, 0),
    )
    mine, other = pl.pallas_call(
        gather_kernel,
        grid_spec=pltpu.PrefetchScalarGridSpec(
            num_scalar_prefetch=1,
            grid=(rows_total,),
            in_specs=[phase_row, vmem],
            out_specs=[sample_block] * 2,
            scratch_shapes=[
                pltpu.VMEM((2, slab * parts, HALF), f32),
                pltpu.VMEM((2, slab * parts, SIDE * clusters), f32),
                pltpu.VMEM((2, high, HEIGHT, clusters), f32),
            ],
        ),
        out_shape=[jax.ShapeDtypeStruct((wide, high, deep, HEIGHT, clusters), f32)] * 2,
        compiler_params=pltpu.CompilerParams(vmem_limit_bytes=24 << 20),
        name="gather",
    )(where, phases, in_vmem(field.reshape(2, parts, G, HALF)))
    sampled = (mine + swapped(other, "core", 1)).reshape(wide * high, deep, HEIGHT, clusters)
    line = sampled[0] + sum(swapped(sampled[o], PLANE, o) for o in range(1, wide * high))
    samples = [line[0]] + [swapped(line[o], "z", o) for o in range(1, deep)]
    samples = [in_vmem(sample) for sample in samples]
    near = near_field(
        density.reshape(3, clusters, panels), near_tiles, pair_target, pair_count
    )
    return pl.pallas_call(
        final_kernel,
        in_specs=[smem] + [vmem] * (2 + deep),
        out_shape=jax.ShapeDtypeStruct(density.shape, f32),
        compiler_params=pltpu.CompilerParams(vmem_limit_bytes=24 << 20),
        name="final",
    )(pair_landing, near, in_vmem(proj_weight), *samples)


def solution(mesh):
    in_specs = (
        P(None, AXES),
        P(None, AXES),
        P(None, AXES),
        P(None, AXES),
        P(AXES, None, None, None, None),
        P(AXES),
        P(AXES),
        P(AXES),
    )
    rows_total, cols_total = (mesh.shape[axis] for axis in ("row", "col"))
    high = cols_total // 2
    wide = high if rows_total % high == 0 else 1
    split_mesh = jax.sharding.Mesh(
        mesh.devices.reshape(rows_total // wide, wide, high, 2), AXES
    )
    return jax.shard_map(
        per_device, mesh=split_mesh, in_specs=in_specs, out_specs=P(None, AXES), check_vma=False
    )
```

```python
import functools
import math

import jax
import jax.numpy as jnp
import numpy as np
from jax import lax
from jax.experimental import pallas as pl
from jax.experimental.pallas import tpu as pltpu
from jax.sharding import PartitionSpec as P

G = 256
HALF = G // 2
STENCIL = 27
SIDE = 3
FINE = 4
SAMPLES = 3 * STENCIL
HEIGHT = 88
TILE = 16
ROW = ("z", "x")
PLANE = ("x", "y")
AXES = ("z", "x", "y", "core")

screen_shift = 0.5


def swapped(values, axes, offset):
    count = lax.axis_size(axes)
    return lax.ppermute(values, axes, [(i, i ^ offset) for i in range(count)])


def in_vmem(values):
    return pltpu.with_memory_space_constraint(values, pltpu.VMEM)


def row_shift(values, by):
    count = lax.axis_size(ROW)
    return lax.ppermute(values, ROW, [(i, (i + by) % count) for i in range(count)])


def near_field(charges, near_tiles, pair_target, pair_count):
    rounded = charges.astype(jnp.bfloat16)
    slot_total = pair_target.shape[0]
    picked = rounded[:, pair_target, :]
    partial_value = jnp.einsum(
        "qabij,aqi->qbj", near_tiles, picked, preferred_element_type=jnp.float32
    )
    live_mask = jnp.arange(slot_total, dtype=jnp.int32) < pair_count[0]
    partial_value = jnp.where(
        live_mask[:, None, None], partial_value, jnp.zeros_like(partial_value)
    )
    return partial_value


def near_exchange(partial_value):
    slot_group, panels = partial_value.shape[0] // 3, partial_value.shape[2]
    leaving = partial_value[slot_group:].reshape(slot_group, 2, 3, panels)
    crossing = jnp.stack([row_shift(leaving[:, 0], -1), row_shift(leaving[:, 1], 1)], axis=1)
    return jnp.concatenate(
        [partial_value[:slot_group], crossing.reshape(2 * slot_group, 3, panels)], axis=0
    )


def half_tables():
    cells = np.arange(HALF)
    parts = []
    for parity in range(2):
        product = cells[:, None] * (2 * cells[None, :] + parity) % G
        angles = product * (2.0 * np.pi / G)
        cosines, sines = np.cos(angles), np.sin(angles)
        table = np.block([[cosines, -sines], [sines, cosines]]).astype(np.float32)
        high = table.astype(jnp.bfloat16)
        low = (table - high.astype(np.float32)).astype(jnp.bfloat16)
        parts.append(np.stack([high, low]))
    return np.stack(parts)


def split(values):
    high = values.astype(jnp.bfloat16)
    low = (values - high.astype(jnp.float32)).astype(jnp.bfloat16)
    return high, low


def dot(left, right):
    return jnp.dot(left, right, preferred_element_type=jnp.float32)


def three_pass(left_high, left_low, right_high, right_low):
    return (
        dot(left_high, right_low) + dot(left_low, right_high) + dot(left_high, right_high)
    )


def spread_kernel(density, weights, corners, out):
    clusters = corners.shape[1]
    panels = density.shape[1] // clusters
    unroll = 8
    lane = lax.broadcasted_iota(jnp.int32, (STENCIL, clusters), 1)

    def some(i, sums):
        for j in range(unroll):
            k = i * unroll + j
            at = pl.ds(pl.multiple_of(k * panels, panels), panels)
            weight = weights[:, at]
            sums = tuple(
                jnp.where(
                    lane == k,
                    jnp.sum(weight * density[a : a + 1, at], axis=1, keepdims=True),
                    sums[a],
                )
                for a in range(3)
            )
        return sums

    blank = jnp.zeros((STENCIL, clusters), jnp.float32)
    sums = lax.fori_loop(0, clusters // unroll, some, (blank, blank, blank))
    for a in range(3):
        out[a * STENCIL : (a + 1) * STENCIL, :] = sums[a]
    out[SAMPLES : SAMPLES + 3, :] = corners[...].astype(jnp.float32)
    out[SAMPLES + 3 :, :] = jnp.zeros((HEIGHT - SAMPLES - 3, clusters), jnp.float32)


def final_kernel(landing, near, weights, *refs):
    *samples, out = refs
    clusters = samples[0].shape[1]
    panels = weights.shape[1] // clusters
    total = sum(sample[...] for sample in samples[1:]) + samples[0][...]
    columns = [total[a * STENCIL : (a + 1) * STENCIL] for a in range(3)]
    for k in range(clusters):
        at = slice(k * panels, (k + 1) * panels)
        weight = weights[:, at]
        for a in range(3):
            out[a : a + 1, at] = jnp.sum(
                columns[a][:, k : k + 1] * weight, axis=0, keepdims=True
            )
    for q in range(near.shape[0]):
        at = pl.ds(pl.multiple_of(landing[q] * panels, panels), panels)
        out[:, at] = out[:, at] + near[q]


def ordered(group, high, step, where, sources, stencils):
    deep = (step // group) ^ where[2]
    for o in range(group * high):

        def fill(o=o):
            y = (o % high) ^ where[4]
            stencils[2 * y + where[0]] = sources[o][deep]
            stencils[2 * y + 1 - where[0]] = sources[group * high + o][deep]

        if group == 1:
            fill()
        else:
            pl.when(step % group == o // high)(fill)


def cosine(turns):
    turns = turns & (G - 1)
    turns = jnp.minimum(turns, G - turns)
    flipped = turns > G // 4
    angle = jnp.where(flipped, G // 2 - turns, turns).astype(jnp.float32) * (2.0 * math.pi / G)
    square = angle * angle
    total = jnp.full_like(square, 1.0 / math.factorial(12))
    for order in (10, 8, 6, 4, 2, 0):
        total = total * square + (-1.0) ** (order // 2) / math.factorial(order)
    return jnp.where(flipped, -total, total)


def regrouped(values, span, left):
    if len(values) == 2:
        turned = [pltpu.roll(value, span, axis=1) for value in values]
        return [
            jnp.where(left, values[0], turned[1]),
            jnp.where(left, turned[0], values[1]),
        ]
    return [
        jnp.concatenate([value[:, i * span : (i + 1) * span] for value in values], axis=1)
        for i in range(len(values))
    ]


def scatter_kernel(live, wide, high, begin, end, where, *refs):
    *sources, out, phases, stencils, total = refs
    step = pl.program_id(0)
    group = end - begin
    row = step // group * wide + ((begin + step % group) ^ where[3])
    sides, parts, _, lanes = out.shape
    cols, _, clusters = stencils.shape
    span = G // cols
    slab = total.shape[2] // (2 * parts) * FINE
    coarse_cells = slab // FINE
    corner = row * slab
    ordered(group, high, step, where, sources[: 2 * group * high], stencils)
    bins = lax.broadcasted_iota(jnp.int32, phases.shape[2:], 0)
    waves = bins // 2 + where[1]
    quarter = bins % 2 * (G // 4)
    kept = bins < 2 * live
    bf16 = jnp.bfloat16
    column = lax.broadcasted_iota(jnp.int32, (TILE, clusters), 0)
    ones = jnp.ones((TILE, clusters), bf16)
    zeros = jnp.zeros((TILE, clusters), bf16)
    for c in range(cols):
        first, second, third = (
            stencils[c, SAMPLES + i : SAMPLES + i + 1, :].astype(jnp.int32) for i in range(3)
        )
        turned = []
        for z in range(SIDE):
            turned.append(jnp.where(kept, cosine((third + z) * waves + quarter), 0.0))
            phases[row * cols + c, z] = turned[z]
        phases[row * cols + c, SIDE, :2] = stencils[c, SAMPLES : SAMPLES + 2, :]
        hots, spreads = [], []
        for x in range(SIDE):
            cell = first - corner + x
            fine = (cell & (FINE - 1)) * span + second - c * span
            fine = jnp.broadcast_to(fine, (TILE, clusters))
            coarse = jnp.broadcast_to(cell // FINE, (TILE, clusters)).astype(jnp.int16)
            for y in range(SIDE):
                target = (fine + y).astype(jnp.int16)
                hots.append(
                    jnp.concatenate(
                        [
                            jnp.where((column + j).astype(jnp.int16) == target, ones, zeros)
                            for j in range(0, FINE * span, TILE)
                        ],
                        axis=0,
                    )
                )
                modes = []
                for a in range(3):
                    at = a * STENCIL + x * 9 + y * 3
                    modes.append(
                        sum(
                            stencils[c, at + z : at + z + 1, :] * turned[z]
                            for z in range(SIDE)
                        )
                    )
                modes = jnp.concatenate(modes, axis=0)
                low = modes - modes.astype(bf16).astype(jnp.float32)
                tile = jnp.concatenate([modes, low], axis=0).astype(bf16)
                pieces = []
                for h in range(coarse_cells):
                    chosen = coarse == jnp.asarray(h, jnp.int16)
                    for j in range(0, 2 * parts, TILE):
                        pieces.append(jnp.where(chosen, tile[j : j + TILE], zeros))
                spreads.append(jnp.concatenate(pieces, axis=0))
        result = lax.dot_general(
            jnp.concatenate(spreads, axis=1),
            jnp.concatenate(hots, axis=1),
            (((1,), (1,)), ((), ())),
            preferred_element_type=jnp.float32,
        )
        for part in range(total.shape[1]):
            total[c, part] = result[:, part * lanes : (part + 1) * lanes]
    across = lanes // span
    left = lax.broadcasted_iota(jnp.int32, (coarse_cells, lanes), 1) < span
    for part in range(total.shape[1]):
        for v in range(parts):
            for side in range(sides):
                values = [
                    total[c, part, pl.ds(v, coarse_cells, stride=2 * parts), :]
                    + total[c, part, pl.ds(parts + v, coarse_cells, stride=2 * parts), :]
                    for c in range(side * across, (side + 1) * across)
                ]
                for i, value in enumerate(regrouped(values, span, left)):
                    at = pl.ds(corner + part * across + i, coarse_cells, stride=FINE)
                    out[side, v, at, :] = value


def dft_kernel(factor, live, pars, where, field, *refs):
    *tables, out, lines, modes = refs
    tx, txt = tables[:2]
    ty, tyt = tables[-2:]
    m = pl.program_id(0)
    width = pars * HALF
    odds = [where[5] + p for p in range(pars)]
    signs = [1.0 - 2.0 * odd.astype(jnp.float32) for odd in odds]

    for p in range(pars):
        for a in range(3):
            values = [field[0, a, m, i] + signs[p] * field[1, a, m, i] for i in range(2)]
            result = three_pass(*split(jnp.concatenate(values, axis=1)), ty[p, 0], ty[p, 1])
            for part in range(2):
                lines[a, part, :, p * HALF : (p + 1) * HALF] = result[
                    :, part * HALF : (part + 1) * HALF
                ]
    for a in range(3):
        for q in range(2):
            values = []
            for part in range(2):
                top, bottom = lines[a, part, :HALF], lines[a, part, HALF:]
                values.append(top - bottom if q else top + bottom)
            result = three_pass(txt[q, 0], txt[q, 1], *split(jnp.concatenate(values, axis=0)))
            for part in range(2):
                modes[a, part, q * HALF : (q + 1) * HALF] = result[
                    part * HALF : (part + 1) * HALF
                ]

    bin_third = where[1] + m
    kthird = bin_third.astype(jnp.float32)
    scale = jnp.where(bin_third == 0, factor, 2.0 * factor)
    scale = jnp.where(m < live, scale, 0.0)
    chunk = 32
    lane = lax.broadcasted_iota(jnp.int32, (1, HALF), 1)
    seconds = []
    for odd in odds:
        bin_second = 2 * lane + odd
        ksecond = jnp.where(bin_second < HALF, bin_second, bin_second - G).astype(jnp.float32)
        seconds.append((ksecond, jnp.where(bin_second == HALF, 0.0, scale)))

    def project(i, carry):
        rows = pl.ds(pl.multiple_of(i * chunk, chunk), chunk)
        at = lax.broadcasted_iota(jnp.int32, (chunk, 1), 0) + i * chunk
        bin_first = jnp.where(at < HALF, 2 * at, 2 * at - (G - 1))
        kfirst = jnp.where(bin_first < HALF, bin_first, bin_first - G).astype(jnp.float32)
        kept = jnp.where(bin_first == HALF, 0.0, 1.0)
        kfirst, kept = (jnp.broadcast_to(k, (chunk, HALF)) for k in (kfirst, kept))
        partly = kfirst * kfirst + kthird * kthird
        for p, (ksecond, weight) in enumerate(seconds):
            at = slice(p * HALF, (p + 1) * HALF)
            squared = partly + ksecond * ksecond
            shifted = squared + screen_shift
            floored = jnp.maximum(squared, 1.0)
            both = 1.0 / (shifted * floored)
            inverse = shifted * both
            weighting = floored * both * (kept * weight)
            for part in range(2):
                u, v, w = (modes[a, part, rows, at] for a in range(3))
                inner = (kfirst * u + ksecond * v + kthird * w) * inverse
                lines[0, part, rows, at] = (u - kfirst * inner) * weighting
                lines[1, part, rows, at] = (v - ksecond * inner) * weighting
                lines[2, part, rows, at] = (w - kthird * inner) * weighting
        return carry

    lax.fori_loop(0, G // chunk, project, 0)

    for a in range(3):
        results = []
        for q in range(2):
            values = [lines[a, part, q * HALF : (q + 1) * HALF] for part in range(2)]
            results.append(
                three_pass(tx[q, 0], tx[q, 1], *split(jnp.concatenate(values, axis=0)))
            )
        for part in range(2):
            even, odd = (r[part * HALF : (part + 1) * HALF] for r in results)
            modes[a, part, :HALF] = even + odd
            modes[a, part, HALF:] = even - odd
    for a in range(3):
        near = far = None
        for p in range(pars):
            values = [modes[a, part, :, p * HALF : (p + 1) * HALF] for part in range(2)]
            result = three_pass(*split(jnp.concatenate(values, axis=1)), tyt[p, 0], tyt[p, 1])
            near = result if near is None else near + result
            far = signs[p] * result if far is None else far + signs[p] * result
        for part in range(2):
            out[0, a, m, part] = near[:, part * HALF : (part + 1) * HALF]
            out[1, a, m, part] = far[:, part * HALF : (part + 1) * HALF]


def gather_kernel(where, phases, field, mine, other, lines, found, results):
    parts = field.shape[1]
    cols, _, _, clusters = phases.shape
    high = mine.shape[1]
    slab = lines.shape[1] // parts
    start_row = pl.multiple_of(pl.program_id(0) * slab, slab)
    bins = parts // 3
    span = G // cols
    corner = (pl.program_id(0) * slab).astype(jnp.float32)
    for side in range(2):
        for v in range(parts):
            lines[side, pl.ds(v, slab, stride=parts), :] = field[side, v, pl.ds(start_row, slab), :]
    halves = [split(lines[side]) for side in range(2)]
    rows = lax.broadcasted_iota(jnp.int32, (2 * span, clusters), 0)
    rows = jnp.where(rows < span, rows, rows - span).astype(jnp.float32)
    for c in range(cols):
        first = phases[c, SIDE, :1] - corner
        second = phases[c, SIDE, 1:2] - c * span
        hot = jnp.concatenate(
            [jnp.where(rows == second + y, 1.0, 0.0) for y in range(SIDE)], axis=1
        ).astype(jnp.bfloat16)
        side, start = divmod(c * span, HALF)
        pair = [half[:, start : start + span] for half in halves[side]]
        found[c % 2] = dot(jnp.concatenate(pair, axis=1), hot)
        target = (c + where[0]) % 2, (c // 2) ^ where[4]
        tall = jnp.broadcast_to(first, (8, clusters))
        for y in range(SIDE):
            lanes = slice(y * clusters, (y + 1) * clusters)
            sums = [[jnp.zeros((8, clusters), jnp.float32)] * (parts // 8) for _ in range(SIDE)]
            chosen = {}
            for cell in range(slab):
                if cell <= slab - SIDE:
                    chosen[cell] = tall == cell
                for j in range(parts // 8):
                    at = cell * parts + j * 8
                    value = found[c % 2, at : at + 8, lanes]
                    for x in range(SIDE):
                        if cell - x in chosen:
                            sums[x][j] = jnp.where(chosen[cell - x], value, sums[x][j])
            for x in range(SIDE):
                total = jnp.concatenate(sums[x], axis=0)
                for a in range(3):
                    mode = total[a * bins : (a + 1) * bins]
                    for z in range(SIDE):
                        at = a * STENCIL + x * 9 + y * 3 + z
                        results[*target, at : at + 1, :] = jnp.sum(
                            mode * phases[c, z], axis=0, keepdims=True
                        )
        results[*target, SAMPLES:, :] = jnp.zeros((HEIGHT - SAMPLES, clusters), jnp.float32)
    for j in range(high):
        mine[0, j, 0] = results[0, j]
        other[0, j, 0] = results[1, j]


def per_device(
    density,
    interp_weight,
    proj_weight,
    stencil_corner,
    near_tiles,
    pair_target,
    pair_landing,
    pair_count,
):
    clusters = stencil_corner.shape[1]
    panels = density.shape[1] // clusters
    deep, wide, high = (lax.axis_size(axis) for axis in AXES[:3])
    here = [lax.axis_index(axis) for axis in AXES]
    rows_total = deep * wide
    cols_total = high * lax.axis_size("core")
    devices = rows_total * cols_total
    device = lax.axis_index(AXES)
    slab = G // rows_total
    kept_bins = G // 2
    third_parts = min(devices, kept_bins)
    second_parts = devices // third_parts
    pars = 2 // second_parts
    third_live = kept_bins // third_parts
    bins = max(4, third_live)
    parts = 3 * 2 * bins
    width = pars * HALF
    f32, bf16 = jnp.float32, jnp.bfloat16

    charges = density.reshape(3, clusters, panels)
    packed = pl.pallas_call(
        spread_kernel,
        out_shape=jax.ShapeDtypeStruct((HEIGHT, clusters), f32),
        name="spread",
    )(density, interp_weight, stencil_corner)
    line = jnp.stack([packed] + [swapped(packed, "z", o) for o in range(1, deep)])
    first_parity = device % second_parts
    tables = half_tables()
    tx = jnp.asarray(tables)
    txt = jnp.asarray(np.ascontiguousarray(np.swapaxes(tables, 2, 3)))
    tables = [tx, txt]
    if pars == 1:
        tables += [lax.dynamic_slice_in_dim(t, first_parity, 1, axis=0) for t in tables]
    tables = [in_vmem(table) for table in tables]
    near = near_field(
        density.reshape(3, clusters, panels), near_tiles, pair_target, pair_count
    )
    line, near, *tables = lax.optimization_barrier((line, near, *tables))
    sources = [line] + [swapped(line, PLANE, o) for o in range(1, wide * high)]

    factor = 1.0 / math.sqrt(density.shape[1] * devices)
    where = jnp.stack(
        [here[3], device // second_parts * third_live, here[0], here[1], here[2], first_parity]
    ).astype(jnp.int32)

    smem = pl.BlockSpec(memory_space=pltpu.SMEM)
    phase_row = pl.BlockSpec(
        (cols_total, SIDE + 1, 2 * bins, clusters), lambda r, where: (r, 0, 0, 0)
    )
    vmem = pl.BlockSpec(memory_space=pltpu.VMEM)
    span = G // cols_total
    filled = ()
    for begin, end in ((0, 1), (1, wide))[: min(2, wide)]:
        lines = sources[begin * high : end * high]
        if begin:
            filled, lines, near = lax.optimization_barrier((filled, lines, near))
            near = near_exchange(near)
        lines += [swapped(values, "core", 1) for values in lines]
        operands = [in_vmem(values) for values in (*lines, *filled)]
        first_filled = 1 + len(lines)
        filled = pl.pallas_call(
            functools.partial(scatter_kernel, third_live, wide, high, begin, end),
            grid=(deep * (end - begin),),
            in_specs=[smem] + [vmem] * len(operands),
            out_specs=[vmem] * 2,
            out_shape=[
                pltpu.VMEM((2, parts, G, HALF), f32),
                pltpu.VMEM((devices, SIDE + 1, 2 * bins, clusters), f32),
            ],
            scratch_shapes=[
                pltpu.VMEM((cols_total, HEIGHT, clusters), f32),
                pltpu.VMEM((cols_total, FINE * span // HALF, slab // FINE * 2 * parts, HALF), f32),
            ],
            input_output_aliases={first_filled + i: i for i in range(len(filled))},
            compiler_params=pltpu.CompilerParams(vmem_limit_bytes=24 << 20),
            name="scatter",
        )(where, *operands)
    if wide == 1:
        near = near_exchange(near)
    field, phases = filled

    field = in_vmem(field.reshape(2, 3, bins, 2, G, HALF))
    field = pl.pallas_call(
        functools.partial(dft_kernel, factor, third_live, pars),
        grid=(bins,),
        in_specs=[smem] + [vmem] * (1 + len(tables)),
        out_specs=vmem,
        out_shape=pltpu.VMEM((2, 3, bins, 2, G, HALF), f32),
        scratch_shapes=[
            pltpu.VMEM((3, 2, G, width), f32),
            pltpu.VMEM((3, 2, G, width), f32),
        ],
        compiler_params=pltpu.CompilerParams(vmem_limit_bytes=24 << 20),
        name="spectral",
    )(where, field, *tables)
    field, near = lax.optimization_barrier((field, near))

    sample_block = pl.BlockSpec(
        (1, high, 1, HEIGHT, clusters),
        lambda r, where: ((r % wide) ^ where[3], 0, (r // wide) ^ where[2], 0, 0),
    )
    mine, other = pl.pallas_call(
        gather_kernel,
        grid_spec=pltpu.PrefetchScalarGridSpec(
            num_scalar_prefetch=1,
            grid=(rows_total,),
            in_specs=[phase_row, vmem],
            out_specs=[sample_block] * 2,
            scratch_shapes=[
                pltpu.VMEM((2, slab * parts, HALF), f32),
                pltpu.VMEM((2, slab * parts, SIDE * clusters), f32),
                pltpu.VMEM((2, high, HEIGHT, clusters), f32),
            ],
        ),
        out_shape=[jax.ShapeDtypeStruct((wide, high, deep, HEIGHT, clusters), f32)] * 2,
        compiler_params=pltpu.CompilerParams(vmem_limit_bytes=24 << 20),
        name="gather",
    )(where, phases, in_vmem(field.reshape(2, parts, G, HALF)))
    sampled = (mine + swapped(other, "core", 1)).reshape(wide * high, deep, HEIGHT, clusters)
    line = sampled[0] + sum(swapped(sampled[o], PLANE, o) for o in range(1, wide * high))
    samples = [line[0]] + [swapped(line[o], "z", o) for o in range(1, deep)]
    samples = [in_vmem(sample) for sample in samples]
    return pl.pallas_call(
        final_kernel,
        in_specs=[smem] + [vmem] * (2 + deep),
        out_shape=jax.ShapeDtypeStruct(density.shape, f32),
        compiler_params=pltpu.CompilerParams(vmem_limit_bytes=24 << 20),
        name="final",
    )(pair_landing, near, in_vmem(proj_weight), *samples)


def solution(mesh):
    in_specs = (
        P(None, AXES),
        P(None, AXES),
        P(None, AXES),
        P(None, AXES),
        P(AXES, None, None, None, None),
        P(AXES),
        P(AXES),
        P(AXES),
    )
    rows_total, cols_total = (mesh.shape[axis] for axis in ("row", "col"))
    high = cols_total // 2
    wide = high if rows_total % high == 0 else 1
    split_mesh = jax.sharding.Mesh(
        mesh.devices.reshape(rows_total // wide, wide, high, 2), AXES
    )
    return jax.shard_map(
        per_device, mesh=split_mesh, in_specs=in_specs, out_specs=P(None, AXES), check_vma=False
    )
```
